32 devices in a mesh: section: 16 (over z, y, core), mp: 2 (over x).
Axes of the slice: x: 2, y: 2, z: 4, core: 2. Of those that a mesh axis runs over, the one named last changes fastest.
Arguments:
- gate_weight: bfloat16 [2, 2048, 5632], P(None, 'section', 'mp'), may hold values from -6 to 6
- up_weight: bfloat16 [2, 2048, 5632], P(None, 'section', 'mp'), may hold values from -6 to 6
- hidden_map: int32 [2048], replicated, may hold values from 0 to 2047, as said below
- ffn_map: int32 [5376], replicated, may hold values from 0 to 5631, as said below
Outputs:
- grown_gate: bfloat16 [2, 2, 2048, 11008], P(None, None, 'section', 'mp')
- grown_up: bfloat16 [2, 2, 2048, 11008], P(None, None, 'section', 'mp')
The draws below stay inside these ranges and needn't reach their ends.
Inputs may be any that keep to these rules, and one draw needn't show every extreme that they name: `hidden_map`: entry i names the old unit copied by new unit 2048 + i. Within each aligned block of 128 entries, at most 8 entries name units of any one block of 128 old units, and some block of old units is named exactly 8 times. `ffn_map`: entry j names the FFN unit of the next layer copied by added unit j % 2688 of FFN block j // 2688. Within each aligned block of 2688 entries, at most 1344 entries name units of any one block of 2816 old FFN units, and in each aligned block some block of old units is named exactly 1344 times.
All inputs are finite; a program needn't handle non-finite values.
Results may differ from the reference program's by a relative error of at most 0.001.
Values may be sent and summed in bfloat16 or wider, within the bound.
No kernel may reach another device: no remote copies, remote signals or barrier semaphores. Data moves between devices by JAX's collectives and lax.ppermute only.
A program may use at most 64 MiB of HBM per device.

```python
import jax
import jax.numpy as jnp

D_OLD = 2048
FF_OLD = 5632
LAYERS = 2
FF_EXTRA = 5376
NARROW = 2816
EXTRA_DEV = 2688
SHARD_ROWS = 128
BLOCKS = 16
N_MP = 2


def draw_hidden_map(key, part):
    owners = jax.vmap(lambda single: jax.random.permutation(single, BLOCKS))(jax.random.split(jax.random.fold_in(key, 7), BLOCKS))
    slots = jnp.arange(SHARD_ROWS) % BLOCKS
    chosen = owners[:, slots]
    within = jax.random.randint(jax.random.fold_in(key, 8), (BLOCKS, SHARD_ROWS), 0, SHARD_ROWS)
    return (chosen * SHARD_ROWS + within).reshape(-1).astype(jnp.int32)


def draw_ffn_map(key, part):
    splits = FF_EXTRA // EXTRA_DEV
    owners = jax.vmap(lambda single: jax.random.permutation(single, splits))(jax.random.split(jax.random.fold_in(key, 5), splits))
    slots = jnp.arange(EXTRA_DEV) % splits
    chosen = owners[:, slots]
    within = jax.random.randint(jax.random.fold_in(key, 6), (splits, EXTRA_DEV), 0, NARROW)
    return (chosen * NARROW + within).reshape(-1).astype(jnp.int32)


def shard_levels(own_key, extent, shards, low, largest):
    def one(axis_at, blocks):
        draws = jax.random.uniform(jax.random.fold_in(jax.random.fold_in(own_key, 6), axis_at), (blocks,), jnp.float32, low / len(shards), largest / len(shards))
        return jnp.repeat(jnp.exp(draws), extent[axis_at] // blocks).reshape((-1,) + (1,) * (len(extent) - axis_at - 1))

    factor_of = one(*shards[0])
    for cut in shards[1:]:
        factor_of = factor_of * one(*cut)
    return factor_of


def scatter_about(stream_key, dims, deviation, limit, cuts=(), kind=jnp.bfloat16):
    array = deviation * jax.random.normal(stream_key, dims, jnp.float32)
    if cuts:
        array = array * shard_levels(stream_key, dims, cuts, -0.22, 0.18)
    return jnp.clip(array, -limit, limit).astype(kind)


def setup_inputs(seed: int = 0) -> dict:
    arg_keys = jax.random.split(jax.random.key(seed), 5)
    return {
        "gate_weight": scatter_about(arg_keys[0], (LAYERS, D_OLD, FF_OLD), 1.0, 6.0, ((1, 16), (2, 2))),
        "up_weight": scatter_about(arg_keys[1], (LAYERS, D_OLD, FF_OLD), 1.0, 6.0, ((1, 16), (2, 2))),
        "hidden_map": draw_hidden_map(jax.random.fold_in(arg_keys[4], 71), 0),
        "ffn_map": draw_ffn_map(jax.random.fold_in(arg_keys[4], 71), 0),
    }


def reference(gate_weight, up_weight, hidden_map, ffn_map):
    layers, d_old, ff_old = gate_weight.shape
    narrow = ff_old // N_MP
    extra_dev = ffn_map.shape[0] // N_MP
    counts = jax.ops.segment_sum(jnp.ones((d_old,), jnp.float32), hidden_map.astype(jnp.int32), num_segments=d_old) + 1.0
    sources = jnp.concatenate([jnp.arange(d_old, dtype=jnp.int32), hidden_map.astype(jnp.int32)])
    divisor = counts[sources].reshape(2, d_old)
    next_layer = jnp.minimum(jnp.arange(layers, dtype=jnp.int32) + 1, layers - 1)

    def widen_matrix(weight):
        rows_taken = jnp.take(weight, sources, axis=1).reshape(layers, 2, d_old, ff_old)
        added = jnp.take(rows_taken[next_layer], ffn_map.astype(jnp.int32), axis=3)
        base_part = rows_taken.reshape(layers, 2, d_old, N_MP, narrow)
        added_part = added.reshape(layers, 2, d_old, N_MP, extra_dev)
        widened = jnp.concatenate([base_part, added_part], axis=4).reshape(layers, 2, d_old, N_MP * (narrow + extra_dev))
        return (widened.astype(jnp.float32) / divisor[None, :, :, None]).astype(jnp.bfloat16)

    return widen_matrix(gate_weight), widen_matrix(up_weight)
```

```python
import functools

import jax
import jax.numpy as jnp
from jax import lax
from jax.experimental import pallas as pl
from jax.experimental.pallas import tpu as pltpu
from jax.sharding import PartitionSpec as P


F32 = jnp.float32
BF16 = jnp.bfloat16
I32 = jnp.int32
VMEM = pl.BlockSpec(memory_space=pltpu.VMEM)
HBM = pl.BlockSpec(memory_space=pl.ANY)
K_CHUNK = 256
PARAMS = pltpu.CompilerParams(vmem_limit_bytes=32 << 20)


def iota(shape, axis):
    return lax.broadcasted_iota(I32, shape, axis)


def count_of(table, ids):
    total = jnp.zeros((ids.shape[0], table.shape[1]), F32)
    for block in range(table.shape[0]):
        total += jnp.where(table[block : block + 1, :] == ids, 1.0, 0.0)
    return 1.0 + jnp.sum(total, axis=1, keepdims=True)


def pick_matrix(table, me, cap, key_ref, within_ref, targets):
    blocks, rows = table.shape
    owner = lax.div(table, jnp.full_like(table, rows))
    within_ref[...] = table - owner * rows
    wanted = owner == me
    before = (iota((rows, rows), 0) < iota((rows, rows), 1)).astype(F32).astype(BF16)
    order = jnp.dot(wanted.astype(F32).astype(BF16), before, preferred_element_type=F32)
    key_ref[...] = jnp.where(wanted, order.astype(I32), -1)
    slot = iota((cap, rows), 0)
    parts = []
    for target in targets:
        line = pl.ds(target, 1)
        parts.append(jnp.where(key_ref[line, :] == slot, within_ref[line, :], 0).astype(F32))
    row_of = jnp.sum(jnp.concatenate(parts, axis=0), axis=1, keepdims=True).astype(I32)
    pick = (iota((blocks * cap, rows), 1) == row_of).astype(F32).astype(BF16)
    return pick, count_of(table, row_of + me * rows)


def land_matrix(mine, blocks, cap):
    rows = mine.shape[1]
    across, down = iota((rows, rows), 1), iota((rows, rows), 0)
    column = jnp.sum(
        jnp.where(across == down, mine, 0).astype(F32), axis=1, keepdims=True
    ).astype(I32)
    owner_row = lax.div(mine, jnp.full_like(mine, rows))
    owner = lax.div(column, jnp.full_like(column, rows))
    earlier = (across < down) & (owner == owner_row)
    rank = jnp.sum(jnp.where(earlier, 1.0, 0.0), axis=1, keepdims=True).astype(I32)
    return (iota((rows, blocks * cap), 1) == owner * cap + rank).astype(F32).astype(BF16)


def onehot_dot(left, index_row, extent):
    total = None
    for start in range(0, extent, K_CHUNK):
        size = min(K_CHUNK, extent - start)
        mask = iota((size, index_row.shape[1]), 0) == index_row - start
        term = jnp.dot(
            left[:, start : start + size],
            mask.astype(F32).astype(BF16),
            preferred_element_type=F32,
        )
        total = term if total is None else total + term
    return total


def send_kernel(layer, cap, halves, table_ref, gate_ref, up_ref, *refs):
    *sent_refs, map_ref, in_ref, held_ref, key_ref, within_ref, map_sem, in_sems, out_sems = refs
    blocks = table_ref.shape[0]
    map_load = pltpu.make_async_copy(table_ref, map_ref, map_sem)
    map_load.start()
    narrow = gate_ref.shape[2]
    steps = in_sems.shape[1]
    width = narrow // steps
    me = lax.axis_index("section")
    loads = []
    for side, ref in enumerate((gate_ref, up_ref)):
        for step in range(steps):
            at = side * narrow + step * width
            loads.append(
                pltpu.make_async_copy(
                    ref.at[layer, :, pl.ds(step * width, width)],
                    in_ref.at[:, pl.ds(at, width)],
                    in_sems.at[side, step],
                )
            )
            loads[-1].start()
    if halves:
        half = blocks // 2
        base = lax.div(me, half) * half
        targets = [base + p for p in range(half)] + [me ^ p for p in range(half, blocks)]
    else:
        targets = list(range(blocks))
    map_load.wait()
    pick, count = pick_matrix(map_ref[...], me, cap, key_ref, within_ref, targets)
    scale = 1.0 / count
    stores = []
    for number, load in enumerate(loads):
        at = number * width
        load.wait()
        rows = jnp.dot(pick, in_ref[:, at : at + width], preferred_element_type=F32)
        held_ref[:, at : at + width] = (rows * scale).astype(BF16)
        first = 0
        for piece, ref in enumerate(sent_refs):
            count_here = ref.shape[0]
            stores.append(
                pltpu.make_async_copy(
                    held_ref.at[pl.ds(first, count_here), pl.ds(at, width)],
                    ref.at[:, pl.ds(at, width)],
                    out_sems.at[number, piece],
                )
            )
            stores[-1].start()
            first += count_here
    for store in stores:
        store.wait()


def send_rows(table, gate, up, layer, cap, halves):
    _, rows, narrow = gate.shape
    blocks = table.shape[0]
    steps = 2
    if halves:
        counts = [blocks // 2 * cap] + [cap] * (blocks // 2)
    else:
        counts = [blocks * cap]
    return pl.pallas_call(
        functools.partial(send_kernel, layer, cap, halves),
        out_shape=[jax.ShapeDtypeStruct((count, 2 * narrow), BF16) for count in counts],
        in_specs=[HBM] * 3,
        out_specs=[HBM] * len(counts),
        scratch_shapes=[
            pltpu.VMEM((blocks, rows), I32),
            pltpu.VMEM((rows, 2 * narrow), BF16),
            pltpu.VMEM((blocks * cap, 2 * narrow), BF16),
            pltpu.VMEM((blocks, rows), I32),
            pltpu.VMEM((blocks, rows), I32),
            pltpu.SemaphoreType.DMA(()),
            pltpu.SemaphoreType.DMA((2, steps)),
            pltpu.SemaphoreType.DMA((2 * steps, len(counts))),
        ],
        cost_estimate=pl.CostEstimate(
            flops=4 * blocks * cap * rows * narrow,
            bytes_accessed=8 * rows * narrow,
            transcendentals=0,
        ),
    )(table, gate, up)


def load_weights(layers, gate_ref, up_ref, in_ref, sems):
    loads = []
    for at, layer in enumerate(layers):
        for side, ref in enumerate((gate_ref, up_ref)):
            loads.append(
                pltpu.make_async_copy(ref.at[layer], in_ref.at[at, side], sems.at[at, side])
            )
            loads[-1].start()
    return loads


def own_kernel(table_ref, ids_ref, gate_ref, up_ref, out_ref, in_ref, own_ref, sems):
    layers, rows, narrow = gate_ref.shape
    loads = load_weights([layers - 1], gate_ref, up_ref, in_ref, sems)
    me = lax.axis_index("section")
    scale = 1.0 / count_of(table_ref[...], iota((rows, 1), 0) + me * rows)
    for side, load in enumerate(loads):
        load.wait()
        own_ref[side * rows : (side + 1) * rows] = (in_ref[0, side].astype(F32) * scale).astype(BF16)
    for s in range(ids_ref.shape[0]):
        out_ref[s] = onehot_dot(own_ref, ids_ref[s : s + 1, :], narrow).astype(BF16)


def own_rows(table, ids, gate, up):
    _, rows, narrow = gate.shape
    turns, width = ids.shape
    return pl.pallas_call(
        own_kernel,
        out_shape=jax.ShapeDtypeStruct((turns, 2 * rows, width), BF16),
        in_specs=[VMEM, VMEM, HBM, HBM],
        out_specs=VMEM,
        scratch_shapes=[
            pltpu.VMEM((1, 2, rows, narrow), BF16),
            pltpu.VMEM((2 * rows, narrow), BF16),
            pltpu.SemaphoreType.DMA((1, 2)),
        ],
        cost_estimate=pl.CostEstimate(
            flops=4 * rows * narrow * width * turns,
            bytes_accessed=8 * rows * narrow,
            transcendentals=0,
        ),
        name="own_rows",
    )(table, ids, gate, up)


def land_kernel(cap, table_ref, land_ref):
    mine = table_ref[pl.ds(lax.axis_index("section"), 1), :]
    land_ref[...] = land_matrix(mine, table_ref.shape[0], cap)


def land_rows(table, cap):
    blocks, rows = table.shape
    return pl.pallas_call(
        functools.partial(land_kernel, cap),
        out_shape=jax.ShapeDtypeStruct((rows, blocks * cap), BF16),
        in_specs=[VMEM],
        out_specs=VMEM,
        compiler_params=PARAMS,
        name="land_rows",
    )(table)


def arrive_kernel(land_ref, ids_ref, *refs):
    *came_refs, rows_ref, out_ref, held_ref, sems = refs
    narrow = rows_ref.shape[1]
    rows = land_ref.shape[0]
    cap = came_refs[1].shape[0]
    half = len(came_refs) - 1
    me = lax.axis_index("section")
    starts = [lax.div(me, half) * half] + [me ^ p for p in range(half, 2 * half)]
    loads = []
    for piece, (ref, start) in enumerate(zip(came_refs, starts)):
        where = pl.ds(pl.multiple_of(start * cap, cap), ref.shape[0])
        loads.append(pltpu.make_async_copy(ref, held_ref.at[where, :], sems.at[piece]))
        loads[-1].start()
    for load in loads:
        load.wait()
    for side in range(2):
        rows_ref[side * rows : (side + 1) * rows] = jnp.dot(
            land_ref[...],
            held_ref[:, side * narrow : (side + 1) * narrow],
            preferred_element_type=F32,
        ).astype(BF16)
    for s in range(ids_ref.shape[0]):
        out_ref[s] = onehot_dot(rows_ref, ids_ref[s : s + 1, :], narrow).astype(BF16)


def arrive_rows(land, ids, came):
    rows, slots = land.shape
    narrow = came[0].shape[1] // 2
    turns, width = ids.shape
    return pl.pallas_call(
        arrive_kernel,
        out_shape=(
            jax.ShapeDtypeStruct((2 * rows, narrow), BF16),
            jax.ShapeDtypeStruct((turns, 2 * rows, width), BF16),
        ),
        in_specs=[VMEM, VMEM] + [HBM] * len(came),
        out_specs=(VMEM,) * 2,
        scratch_shapes=[
            pltpu.VMEM((slots, 2 * narrow), BF16),
            pltpu.SemaphoreType.DMA((len(came),)),
        ],
        compiler_params=PARAMS,
        cost_estimate=pl.CostEstimate(
            flops=4 * rows * narrow * width * turns,
            bytes_accessed=8 * rows * narrow,
            transcendentals=0,
        ),
        name="arrive_rows",
    )(land, ids, *came)


def near_kernel(rows_ref, ids_ref, out_ref):
    for start, size in column_tiles(ids_ref.shape[1]):
        out_ref[:, start : start + size] = onehot_dot(
            rows_ref, ids_ref[:, start : start + size], rows_ref.shape[1]
        ).astype(BF16)


def near_columns(rows, ids):
    count, narrow = rows.shape
    extra = ids.shape[1]
    return pl.pallas_call(
        near_kernel,
        out_shape=jax.ShapeDtypeStruct((count, extra), BF16),
        in_specs=[VMEM] * 2,
        out_specs=VMEM,
        compiler_params=PARAMS,
        cost_estimate=pl.CostEstimate(
            flops=2 * count * narrow * extra,
            bytes_accessed=2 * count * (narrow + extra),
            transcendentals=0,
        ),
    )(rows, ids)


def column_tiles(extent):
    pieces = -(-extent // 1408)
    size = extent // pieces // 256 * 256 or extent
    starts = [size * piece for piece in range(pieces)]
    return [
        (start, (extent if start == starts[-1] else start + size) - start) for start in starts
    ]


def put_extras(half, narrow, near, far_ref, ids_ref, outs, held_ref, sems):
    rows = held_ref.shape[0] // len(outs)
    layers = outs[0].shape[0]
    copies = []
    for step, (start, size) in enumerate(column_tiles(held_ref.shape[1])):
        total = None
        for s in range(ids_ref.shape[0]):
            far = onehot_dot(far_ref.at[s], ids_ref[s : s + 1, start : start + size], far_ref.shape[2])
            total = far if total is None else total + far
        held_ref[:, start : start + size] = (total + near(start, size)).astype(BF16)
        for layer in range(layers):
            for side, out in enumerate(outs):
                copies.append(
                    pltpu.make_async_copy(
                        held_ref.at[pl.ds(side * rows, rows), pl.ds(start, size)],
                        out.at[layer, half, :, pl.ds(narrow + start, size)],
                        sems.at[step, layer, side],
                    )
                )
                copies[-1].start()
    return copies


def first_kernel(
    table_ref, near_ids_ref, far_ref, far_ids_ref, gate_ref, up_ref, gate_out, up_out,
    in_ref, base_ref, held_ref, in_sems, base_sems, sems,
):
    layers, rows, narrow = gate_ref.shape
    order = list(range(layers))[::-1]
    loads = load_weights(order, gate_ref, up_ref, in_ref, in_sems)
    scale = 1.0 / count_of(
        table_ref[...], iota((rows, 1), 0) + lax.axis_index("section") * rows
    )
    outs = (gate_out, up_out)
    copies = []
    for number, load in enumerate(loads):
        at, side = number // 2, number % 2
        load.wait()
        here = pl.ds(side * rows, rows)
        base_ref[at, here] = (in_ref[at, side].astype(F32) * scale).astype(BF16)
        copies.append(
            pltpu.make_async_copy(
                base_ref.at[at, here],
                outs[side].at[order[at], 0, :, pl.ds(0, narrow)],
                base_sems.at[at, side],
            )
        )
        copies[-1].start()

    def near(start, size):
        return onehot_dot(base_ref.at[0], near_ids_ref[:, start : start + size], narrow)

    copies += put_extras(0, narrow, near, far_ref, far_ids_ref, outs, held_ref, sems)
    for copy in copies:
        copy.wait()


def first_half(table, near_ids, far, far_ids, gate, up, out_type):
    layers, rows, narrow = gate.shape
    extra = near_ids.shape[1]
    return pl.pallas_call(
        first_kernel,
        out_shape=(out_type, out_type),
        in_specs=[VMEM] * 4 + [HBM] * 2,
        out_specs=(HBM, HBM),
        scratch_shapes=[
            pltpu.VMEM((layers, 2, rows, narrow), BF16),
            pltpu.VMEM((layers, 2 * rows, narrow), BF16),
            pltpu.VMEM((2 * rows, extra), BF16),
            pltpu.SemaphoreType.DMA((layers, 2)),
            pltpu.SemaphoreType.DMA((layers, 2)),
            pltpu.SemaphoreType.DMA((len(column_tiles(extra)), layers, 2)),
        ],
        compiler_params=PARAMS,
        cost_estimate=pl.CostEstimate(
            flops=4 * rows * (narrow + far.shape[2] * far.shape[0]) * extra,
            bytes_accessed=8 * layers * rows * (narrow + extra),
            transcendentals=0,
        ),
        name="first_half",
    )(table, near_ids, far, far_ids, gate, up)


def second_kernel(
    rows_ref, near_ref, far_ref, ids_ref, gate_in, up_in, gate_out, up_out,
    held_ref, base_sems, sems,
):
    rows, narrow = rows_ref.shape[0] // 2, rows_ref.shape[1]
    outs = (gate_out, up_out)
    layers = gate_out.shape[0]
    copies = []
    for side, out in enumerate(outs):
        copies.append(
            pltpu.make_async_copy(
                rows_ref.at[pl.ds(side * rows, rows), :],
                out.at[layers - 1, 1, :, pl.ds(0, narrow)],
                base_sems.at[side],
            )
        )
        copies[-1].start()

    def near(start, size):
        return near_ref[:, start : start + size].astype(F32)

    copies += put_extras(1, narrow, near, far_ref, ids_ref, outs, held_ref, sems)
    for copy in copies:
        copy.wait()


def second_half(rows, near, far, ids, gate_out, up_out):
    count, narrow = rows.shape
    extra = near.shape[1]
    layers = gate_out.shape[0]
    out_type = jax.ShapeDtypeStruct(gate_out.shape, BF16)
    return pl.pallas_call(
        second_kernel,
        out_shape=(out_type, out_type),
        in_specs=[VMEM] * 4 + [HBM] * 2,
        out_specs=(HBM, HBM),
        input_output_aliases={4: 0, 5: 1},
        scratch_shapes=[
            pltpu.VMEM((count, extra), BF16),
            pltpu.SemaphoreType.DMA((2,)),
            pltpu.SemaphoreType.DMA((len(column_tiles(extra)), layers, 2)),
        ],
        compiler_params=PARAMS,
        cost_estimate=pl.CostEstimate(
            flops=2 * count * far.shape[2] * far.shape[0] * extra,
            bytes_accessed=4 * count * (narrow + layers * extra),
            transcendentals=0,
        ),
        name="second_half",
    )(rows, near, far, ids, gate_out, up_out)


def last_kernel(
    land_ref, came_ref, gate_in, up_in, gate_out, up_out, in_ref, held_ref, in_sems, out_sems
):
    narrow = came_ref.shape[1] // 2
    steps = in_sems.shape[1]
    width = narrow // steps
    loads, stores = [], []
    for number in range(2 * steps):
        columns = pl.ds(number * width, width)
        loads.append(
            pltpu.make_async_copy(
                came_ref.at[:, columns],
                in_ref.at[:, columns],
                in_sems.at[number // steps, number % steps],
            )
        )
        loads[-1].start()
    for side, out in enumerate((gate_out, up_out)):
        for step in range(steps):
            at = side * narrow + step * width
            loads[side * steps + step].wait()
            held_ref[:, at : at + width] = jnp.dot(
                land_ref[...], in_ref[:, at : at + width], preferred_element_type=F32
            ).astype(BF16)
            stores.append(
                pltpu.make_async_copy(
                    held_ref.at[:, pl.ds(at, width)],
                    out.at[0, 1, :, pl.ds(step * width, width)],
                    out_sems.at[side, step],
                )
            )
            stores[-1].start()
    for store in stores:
        store.wait()


def last_rows(land, came, gate_out, up_out):
    rows, slots = land.shape
    narrow = came.shape[1] // 2
    steps = 2
    out_type = jax.ShapeDtypeStruct(gate_out.shape, BF16)
    return pl.pallas_call(
        last_kernel,
        out_shape=(out_type, out_type),
        in_specs=[VMEM] + [HBM] * 3,
        out_specs=(HBM, HBM),
        input_output_aliases={2: 0, 3: 1},
        scratch_shapes=[
            pltpu.VMEM((slots, 2 * narrow), BF16),
            pltpu.VMEM((rows, 2 * narrow), BF16),
            pltpu.SemaphoreType.DMA((2, steps)),
            pltpu.SemaphoreType.DMA((2, steps)),
        ],
        compiler_params=PARAMS,
        cost_estimate=pl.CostEstimate(
            flops=4 * rows * slots * narrow,
            bytes_accessed=8 * rows * narrow,
            transcendentals=0,
        ),
        name="last_rows",
    )(land, came, gate_out, up_out)


def column_plan(ffn_map, splits, narrow, width):
    rank = lax.axis_index("mp")
    extra = ffn_map.shape[0] // splits
    table = ffn_map.reshape(splits, extra)
    owner = table // narrow
    within = table - owner * narrow

    def line(array, at):
        return lax.dynamic_index_in_dim(array, at, 0, keepdims=False)

    my_owner, my_within = line(owner, rank), line(within, rank)
    near = jnp.where(my_owner == rank, my_within, -1)[None, :]
    turns = range(1, splits)
    targets = [lax.rem(rank + turn, splits) for turn in turns]
    origins = [lax.rem(rank + splits - turn, splits) for turn in turns]
    hits = jnp.stack(
        [line(owner, target) == rank for target in targets]
        + [my_owner == origin for origin in origins]
    )
    order = jnp.where(hits, jnp.cumsum(hits.astype(I32), axis=1) - 1, -1)
    slots = jnp.arange(width, dtype=I32)
    sends = [
        jnp.sum(
            jnp.where(order[at][None, :] == slots[:, None], line(within, target)[None, :] + 1, 0),
            axis=1,
        )
        - 1
        for at, target in enumerate(targets)
    ]
    return near, jnp.stack(sends), order[splits - 1 :]


def turn_around(sent, splits):
    return jnp.stack(
        [
            lax.ppermute(sent[turn - 1], "mp", [(i, (i + turn) % splits) for i in range(splits)])
            for turn in range(1, splits)
        ]
    )


def tiled_local(gate_weight, up_weight, hidden_map, ffn_map):
    layers, rows, narrow = gate_weight.shape
    blocks = lax.axis_size("section")
    splits = lax.axis_size("mp")
    extra = ffn_map.shape[0] // splits
    cap = rows // blocks
    column_cap = extra // splits
    width = -(-column_cap // 128) * 128
    table = hidden_map.reshape(blocks, rows)
    out_type = jax.ShapeDtypeStruct((layers, 2, rows, narrow + extra), BF16)

    half = blocks // 2
    groups = [list(range(half)), list(range(half, blocks))]

    def swap_rows(sent, groups=None):
        return lax.all_to_all(
            sent, "section", split_axis=0, concat_axis=0, tiled=True, axis_index_groups=groups
        )

    def cross(sent, p):
        return lax.ppermute(sent, "section", [(i, i ^ p) for i in range(blocks)])

    sent_top = send_rows(table, gate_weight, up_weight, layers - 1, cap, True)
    came_top = [cross(sent_top[1 + p], half + p) for p in range(half)]
    came_top.insert(0, swap_rows(sent_top[0], groups))
    sent_top = sent_top[0]
    ffn_map, table = lax.optimization_barrier((ffn_map, sent_top, table))[::2]
    near_ids, send_ids, far_ids = column_plan(ffn_map, splits, narrow, width)
    own_sent = own_rows(table, send_ids, gate_weight, up_weight)
    own_far = turn_around(own_sent, splits)
    sent_low = send_rows(table, gate_weight, up_weight, 0, cap, False)[0]
    came_low = swap_rows(sent_low)
    land = land_rows(table, cap)
    got, got_sent = arrive_rows(land, send_ids, came_top)
    got_far = turn_around(got_sent, splits)
    outs = first_half(table, near_ids, own_far, far_ids, gate_weight, up_weight, out_type)
    got_near = near_columns(got, near_ids)
    outs = second_half(got, got_near, got_far, far_ids, *outs)
    return last_rows(land, came_low, *outs)


def plain_local(gate_weight, up_weight, hidden_map, ffn_map):
    layers, shard_rows, _ = gate_weight.shape
    blocks = lax.axis_size("section")
    splits = lax.axis_size("mp")
    section_rank = lax.axis_index("section")
    column_rank = lax.axis_index("mp")
    d_old = shard_rows * blocks
    extra_dev = ffn_map.shape[0] // splits
    route_cap = max(1, shard_rows // blocks)
    next_pick = jnp.minimum(jnp.arange(layers, dtype=jnp.int32) + 1, layers - 1) - 1
    counts = (
        jax.ops.segment_sum(jnp.ones((d_old,), jnp.float32), hidden_map, num_segments=d_old) + 1.0
    )
    own_rows = section_rank * shard_rows + jnp.arange(shard_rows, dtype=jnp.int32)
    copied = lax.dynamic_slice_in_dim(hidden_map, section_rank * shard_rows, shard_rows)
    mine_extra = lax.dynamic_slice_in_dim(ffn_map, column_rank * extra_dev, extra_dev)
    table = hidden_map.reshape(blocks, shard_rows)
    owner = table // shard_rows
    wanted = owner == section_rank
    order = jnp.cumsum(wanted.astype(jnp.int32), axis=1) - 1
    slot_ids = jnp.arange(route_cap, dtype=jnp.int32)
    selected = wanted[:, None, :] & (order[:, None, :] == slot_ids[None, :, None])
    sent_rows = jnp.sum(jnp.where(selected, (table % shard_rows)[:, None, :], 0), axis=2).reshape(
        -1
    )
    mine_owner = copied // shard_rows
    row_ids = jnp.arange(shard_rows, dtype=jnp.int32)
    earlier = row_ids[None, :] < row_ids[:, None]
    rank_among = jnp.sum(
        (earlier & (mine_owner[None, :] == mine_owner[:, None])).astype(jnp.int32), axis=1
    )
    landing = mine_owner * route_cap + rank_among
    pair = (gate_weight, up_weight)
    later = tuple((portion[1:] for portion in pair))
    rows_here = pair[0].shape[1]

    def pick_columns(carried, pieces):
        amount = pieces[0].shape[2]
        inside = (mine_extra >= 0) & (mine_extra < amount)
        bounded = jnp.clip(mine_extra, 0, amount - 1)
        return tuple(
            (
                jnp.where(inside, jnp.take(portion, bounded, axis=2), current)
                for current, portion in zip(carried, pieces)
            )
        )

    empty_extra = jnp.zeros((layers - 1, rows_here, extra_dev), jnp.bfloat16)
    extras = pick_columns(
        (empty_extra, empty_extra),
        (
            lax.all_gather(later[0], "mp", axis=2, tiled=True),
            lax.all_gather(later[1], "mp", axis=2, tiled=True),
        ),
    )
    own_gate, own_up = tuple(
        (
            jnp.concatenate([portion, added[next_pick]], axis=2)
            for portion, added in zip(pair, extras)
        )
    )
    arrived = (
        lax.all_to_all(
            jnp.take(own_gate, sent_rows, axis=1),
            "section",
            split_axis=1,
            concat_axis=1,
            tiled=True,
        ),
        lax.all_to_all(
            jnp.take(own_up, sent_rows, axis=1), "section", split_axis=1, concat_axis=1, tiled=True
        ),
    )
    grown_gate = jnp.stack([own_gate, jnp.take(arrived[0], landing, axis=1)], axis=1)
    grown_up = jnp.stack([own_up, jnp.take(arrived[1], landing, axis=1)], axis=1)
    divisor = jnp.stack([counts[own_rows], counts[copied]])[None, :, :, None]
    return (
        (grown_gate.astype(jnp.float32) / divisor).astype(jnp.bfloat16),
        (grown_up.astype(jnp.float32) / divisor).astype(jnp.bfloat16),
    )


def local(gate_weight, up_weight, hidden_map, ffn_map):
    layers, rows, narrow = gate_weight.shape
    blocks = lax.axis_size("section")
    splits = lax.axis_size("mp")
    extra = ffn_map.shape[0] // splits
    whole_tiles = (
        layers == 2
        and splits > 1
        and blocks > 1
        and blocks & (blocks - 1) == 0
        and rows % (8 * blocks) == 0
        and rows % 16 == 0
        and narrow % 256 == 0
        and extra % 128 == 0
        and extra % splits == 0
    )
    form = tiled_local if whole_tiles else plain_local
    return form(gate_weight, up_weight, hidden_map, ffn_map)


def solution(mesh):
    in_specs = (P(None, "section", "mp"), P(None, "section", "mp"), P(), P())
    out_specs = (P(None, None, "section", "mp"), P(None, None, "section", "mp"))
    return jax.shard_map(local, mesh=mesh, in_specs=in_specs, out_specs=out_specs, check_vma=False)
```

```python
import functools

import jax
import jax.numpy as jnp
from jax import lax
from jax.experimental import pallas as pl
from jax.experimental.pallas import tpu as pltpu
from jax.sharding import PartitionSpec as P


F32 = jnp.float32
BF16 = jnp.bfloat16
I32 = jnp.int32
VMEM = pl.BlockSpec(memory_space=pltpu.VMEM)
HBM = pl.BlockSpec(memory_space=pl.ANY)
K_CHUNK = 256
PARAMS = pltpu.CompilerParams(vmem_limit_bytes=32 << 20)


def iota(shape, axis):
    return lax.broadcasted_iota(I32, shape, axis)


def count_of(table, ids):
    total = jnp.zeros((ids.shape[0], table.shape[1]), F32)
    for block in range(table.shape[0]):
        total += jnp.where(table[block : block + 1, :] == ids, 1.0, 0.0)
    return 1.0 + jnp.sum(total, axis=1, keepdims=True)


def pick_matrix(table, me, cap, key_ref, within_ref, targets):
    blocks, rows = table.shape
    owner = lax.div(table, jnp.full_like(table, rows))
    within_ref[...] = table - owner * rows
    wanted = owner == me
    before = (iota((rows, rows), 0) < iota((rows, rows), 1)).astype(F32).astype(BF16)
    order = jnp.dot(wanted.astype(F32).astype(BF16), before, preferred_element_type=F32)
    key_ref[...] = jnp.where(wanted, order.astype(I32), -1)
    slot = iota((cap, rows), 0)
    parts = []
    for target in targets:
        line = pl.ds(target, 1)
        parts.append(jnp.where(key_ref[line, :] == slot, within_ref[line, :], 0).astype(F32))
    row_of = jnp.sum(jnp.concatenate(parts, axis=0), axis=1, keepdims=True).astype(I32)
    pick = (iota((blocks * cap, rows), 1) == row_of).astype(F32).astype(BF16)
    return pick, count_of(table, row_of + me * rows)


def land_matrix(mine, blocks, cap):
    rows = mine.shape[1]
    across, down = iota((rows, rows), 1), iota((rows, rows), 0)
    column = jnp.sum(
        jnp.where(across == down, mine, 0).astype(F32), axis=1, keepdims=True
    ).astype(I32)
    owner_row = lax.div(mine, jnp.full_like(mine, rows))
    owner = lax.div(column, jnp.full_like(column, rows))
    earlier = (across < down) & (owner == owner_row)
    rank = jnp.sum(jnp.where(earlier, 1.0, 0.0), axis=1, keepdims=True).astype(I32)
    return (iota((rows, blocks * cap), 1) == owner * cap + rank).astype(F32).astype(BF16)


def onehot_dot(left, index_row, extent):
    total = None
    for start in range(0, extent, K_CHUNK):
        size = min(K_CHUNK, extent - start)
        mask = iota((size, index_row.shape[1]), 0) == index_row - start
        term = jnp.dot(
            left[:, start : start + size],
            mask.astype(F32).astype(BF16),
            preferred_element_type=F32,
        )
        total = term if total is None else total + term
    return total


def load_weights(layers, gate_ref, up_ref, in_ref, sems):
    narrow = gate_ref.shape[2]
    loads = []
    for at, layer in enumerate(layers):
        for side, ref in enumerate((gate_ref, up_ref)):
            loads.append(
                pltpu.make_async_copy(
                    ref.at[layer],
                    in_ref.at[at, :, pl.ds(side * narrow, narrow)],
                    sems.at[at, side],
                )
            )
            loads[-1].start()
    return loads


def put_slots(loads, pick, scale, in_ref, held_ref, sent_refs, sems):
    width = held_ref.shape[1] // len(loads)
    stores = []
    for side, load in enumerate(loads):
        columns = pl.ds(side * width, width)
        load.wait()
        rows = jnp.dot(pick, in_ref[:, columns], preferred_element_type=F32)
        held_ref[:, columns] = (rows * scale).astype(BF16)
        first = 0
        for piece, ref in enumerate(sent_refs):
            count = ref.shape[0]
            stores.append(
                pltpu.make_async_copy(
                    held_ref.at[pl.ds(first, count), columns],
                    ref.at[:, columns],
                    sems.at[side, piece],
                )
            )
            stores[-1].start()
            first += count
    return stores


def send_kernel(layer, cap, table_ref, gate_ref, up_ref, *refs):
    *sent_refs, map_ref, in_ref, held_ref, key_ref, within_ref, map_sem, in_sems, out_sems = refs
    map_load = pltpu.make_async_copy(table_ref, map_ref, map_sem)
    map_load.start()
    loads = load_weights([layer], gate_ref, up_ref, in_ref, in_sems)
    me = lax.axis_index("section")
    targets = [me ^ p for p in range(map_ref.shape[0])]
    map_load.wait()
    pick, count = pick_matrix(map_ref[...], me, cap, key_ref, within_ref, targets)
    stores = put_slots(loads, pick, 1.0 / count, in_ref.at[0], held_ref, sent_refs, out_sems)
    for store in stores:
        store.wait()


def send_rows(table, gate, up, layer, cap):
    _, rows, narrow = gate.shape
    blocks = table.shape[0]
    return pl.pallas_call(
        functools.partial(send_kernel, layer, cap),
        out_shape=[jax.ShapeDtypeStruct((cap, 2 * narrow), BF16)] * blocks,
        in_specs=[HBM] * 3,
        out_specs=[HBM] * blocks,
        scratch_shapes=[
            pltpu.VMEM((blocks, rows), I32),
            pltpu.VMEM((1, rows, 2 * narrow), BF16),
            pltpu.VMEM((blocks * cap, 2 * narrow), BF16),
            pltpu.VMEM((blocks, rows), I32),
            pltpu.VMEM((blocks, rows), I32),
            pltpu.SemaphoreType.DMA(()),
            pltpu.SemaphoreType.DMA((1, 2)),
            pltpu.SemaphoreType.DMA((2, blocks)),
        ],
        cost_estimate=pl.CostEstimate(
            flops=4 * blocks * cap * rows * narrow,
            bytes_accessed=8 * rows * narrow,
            transcendentals=0,
        ),
        name="send_rows",
    )(table, gate, up)


def running_order(hit):
    lines, lanes = hit.shape
    ones = hit.astype(F32)
    before = (iota((lanes, lanes), 0) < iota((lanes, lanes), 1)).astype(F32).astype(BF16)
    above = (iota((lines, lines), 1) < iota((lines, lines), 0)).astype(F32).astype(BF16)
    sums = jnp.broadcast_to(jnp.sum(ones, axis=1, keepdims=True), (lines, lanes))
    total = jnp.dot(ones.astype(BF16), before, preferred_element_type=F32) + jnp.dot(
        above, sums.astype(BF16), preferred_element_type=F32
    )
    return jnp.where(hit, total.astype(I32), -1)


def column_plan(narrow, map_ref, near_ref, send_ref, far_ref, splits):
    rank = lax.axis_index("mp")
    lines = map_ref.shape[0] // splits
    lanes = map_ref.shape[1]
    width = send_ref.shape[1]
    blocks = [map_ref[split * lines : (split + 1) * lines, :] for split in range(splits)]

    def block_of(index):
        chosen = blocks[0]
        for split in range(1, splits):
            chosen = jnp.where(index == split, blocks[split], chosen)
        owner = lax.div(chosen, jnp.full_like(chosen, narrow))
        return owner, chosen - owner * narrow

    def flatten(value, ref, at):
        for line in range(lines):
            ref[at : at + 1, line * lanes : (line + 1) * lanes] = value[line : line + 1, :]

    owner, within = block_of(rank)
    flatten(jnp.where(owner == rank, within, -1), near_ref, 0)
    for turn in range(1, splits):
        flatten(
            running_order(owner == lax.rem(rank + splits - turn, splits)), far_ref, turn - 1
        )
        their_owner, their_within = block_of(lax.rem(rank + turn, splits))
        key = running_order(their_owner == rank)
        value = (their_within + 1).astype(F32)
        for start in range(0, width, lanes):
            slot = iota((lanes, lanes), 0) + start
            held = jnp.zeros((lanes, lanes), F32)
            for line in range(lines):
                held = jnp.where(key[line : line + 1, :] == slot, value[line : line + 1, :], held)
            column = jnp.sum(held, axis=1, keepdims=True)
            diagonal = iota((lanes, lanes), 0) == iota((lanes, lanes), 1)
            send_ref[turn - 1 : turn, start : start + lanes] = (
                jnp.sum(jnp.where(diagonal, column, 0.0), axis=0, keepdims=True).astype(I32) - 1
            )


def middle_kernel(
    cap, splits, table_ref, map_ref, gate_ref, up_ref, turn_ref, near_ref, send_ref, far_ref, sent_ref,
    in_ref, own_ref, held_ref, key_ref, within_ref, in_sems, out_sems,
):
    layers, rows, narrow = gate_ref.shape
    loads = load_weights([layers - 1, 0], gate_ref, up_ref, in_ref, in_sems)
    me = lax.axis_index("section")
    table = table_ref[...]
    column_plan(narrow, map_ref, near_ref, send_ref, far_ref, splits)
    scale = 1.0 / count_of(table, iota((rows, 1), 0) + me * rows)
    pick, count = pick_matrix(table, me, cap, key_ref, within_ref, list(range(table.shape[0])))
    stores = put_slots(
        loads[2:], pick, 1.0 / count, in_ref.at[1], held_ref, (sent_ref,), out_sems
    )
    for side, load in enumerate(loads[:2]):
        load.wait()
        columns = in_ref[0, :, side * narrow : (side + 1) * narrow]
        own_ref[side * rows : (side + 1) * rows] = (columns.astype(F32) * scale).astype(BF16)
    for s in range(splits - 1):
        turn_ref[s] = onehot_dot(own_ref, send_ref[s : s + 1, :], narrow).astype(BF16)
    for store in stores:
        store.wait()


def middle(table, columns, gate, up, cap, splits, width):
    _, rows, narrow = gate.shape
    blocks = table.shape[0]
    extra = columns.size // splits
    return pl.pallas_call(
        functools.partial(middle_kernel, cap, splits),
        out_shape=(
            jax.ShapeDtypeStruct((splits - 1, 2 * rows, width), BF16),
            jax.ShapeDtypeStruct((1, extra), I32),
            jax.ShapeDtypeStruct((splits - 1, width), I32),
            jax.ShapeDtypeStruct((splits - 1, extra), I32),
            jax.ShapeDtypeStruct((blocks * cap, 2 * narrow), BF16),
        ),
        in_specs=[VMEM, VMEM, HBM, HBM],
        out_specs=(VMEM, VMEM, VMEM, VMEM, HBM),
        scratch_shapes=[
            pltpu.VMEM((2, rows, 2 * narrow), BF16),
            pltpu.VMEM((2 * rows, narrow), BF16),
            pltpu.VMEM((blocks * cap, 2 * narrow), BF16),
            pltpu.VMEM((blocks, rows), I32),
            pltpu.VMEM((blocks, rows), I32),
            pltpu.SemaphoreType.DMA((2, 2)),
            pltpu.SemaphoreType.DMA((2, 1)),
        ],
        cost_estimate=pl.CostEstimate(
            flops=4 * rows * narrow * width,
            bytes_accessed=16 * rows * narrow,
            transcendentals=0,
        ),
        name="middle",
    )(table, columns, gate, up)


def land_kernel(cap, table_ref, land_ref):
    mine = table_ref[pl.ds(lax.axis_index("section"), 1), :]
    land_ref[...] = land_matrix(mine, table_ref.shape[0], cap)


def land_rows(table, cap):
    blocks, rows = table.shape
    return pl.pallas_call(
        functools.partial(land_kernel, cap),
        out_shape=jax.ShapeDtypeStruct((rows, blocks * cap), BF16),
        in_specs=[VMEM],
        out_specs=VMEM,
        compiler_params=PARAMS,
        name="land_rows",
    )(table)


def arrive_kernel(land_ref, ids_ref, *refs):
    *came_refs, rows_ref, out_ref, held_ref, sems = refs
    narrow = rows_ref.shape[1]
    rows = land_ref.shape[0]
    cap = came_refs[0].shape[0]
    me = lax.axis_index("section")
    starts = [me ^ p for p in range(len(came_refs))]
    loads = []
    for piece, (ref, start) in enumerate(zip(came_refs, starts)):
        where = pl.ds(pl.multiple_of(start * cap, cap), ref.shape[0])
        loads.append(pltpu.make_async_copy(ref, held_ref.at[where, :], sems.at[piece]))
        loads[-1].start()
    for load in loads:
        load.wait()
    for side in range(2):
        rows_ref[side * rows : (side + 1) * rows] = jnp.dot(
            land_ref[...],
            held_ref[:, side * narrow : (side + 1) * narrow],
            preferred_element_type=F32,
        ).astype(BF16)
    for s in range(ids_ref.shape[0]):
        out_ref[s] = onehot_dot(rows_ref, ids_ref[s : s + 1, :], narrow).astype(BF16)


def arrive_rows(land, ids, came):
    rows, slots = land.shape
    narrow = came[0].shape[1] // 2
    turns, width = ids.shape
    return pl.pallas_call(
        arrive_kernel,
        out_shape=(
            jax.ShapeDtypeStruct((2 * rows, narrow), BF16),
            jax.ShapeDtypeStruct((turns, 2 * rows, width), BF16),
        ),
        in_specs=[VMEM, VMEM] + [HBM] * len(came),
        out_specs=(VMEM,) * 2,
        scratch_shapes=[
            pltpu.VMEM((slots, 2 * narrow), BF16),
            pltpu.SemaphoreType.DMA((len(came),)),
        ],
        compiler_params=PARAMS,
        cost_estimate=pl.CostEstimate(
            flops=4 * rows * narrow * width * turns,
            bytes_accessed=8 * rows * narrow,
            transcendentals=0,
        ),
        name="arrive_rows",
    )(land, ids, *came)


def near_kernel(rows_ref, ids_ref, out_ref):
    for start, size in column_tiles(ids_ref.shape[1]):
        out_ref[:, start : start + size] = onehot_dot(
            rows_ref, ids_ref[:, start : start + size], rows_ref.shape[1]
        ).astype(BF16)


def near_columns(rows, ids):
    count, narrow = rows.shape
    extra = ids.shape[1]
    return pl.pallas_call(
        near_kernel,
        out_shape=jax.ShapeDtypeStruct((count, extra), BF16),
        in_specs=[VMEM] * 2,
        out_specs=VMEM,
        compiler_params=PARAMS,
        cost_estimate=pl.CostEstimate(
            flops=2 * count * narrow * extra,
            bytes_accessed=2 * count * (narrow + extra),
            transcendentals=0,
        ),
    )(rows, ids)


def column_tiles(extent):
    pieces = -(-extent // 1408)
    size = extent // pieces // 256 * 256 or extent
    starts = [size * piece for piece in range(pieces)]
    return [
        (start, (extent if start == starts[-1] else start + size) - start) for start in starts
    ]


def put_extras(half, narrow, near, far_ref, ids_ref, outs, held_ref, sems):
    rows = held_ref.shape[0] // len(outs)
    layers = outs[0].shape[0]
    copies = []
    for step, (start, size) in enumerate(column_tiles(held_ref.shape[1])):
        total = None
        for s in range(ids_ref.shape[0]):
            far = onehot_dot(far_ref.at[s], ids_ref[s : s + 1, start : start + size], far_ref.shape[2])
            total = far if total is None else total + far
        held_ref[:, start : start + size] = (total + near(start, size)).astype(BF16)
        for layer in range(layers):
            for side, out in enumerate(outs):
                copies.append(
                    pltpu.make_async_copy(
                        held_ref.at[pl.ds(side * rows, rows), pl.ds(start, size)],
                        out.at[layer, half, :, pl.ds(narrow + start, size)],
                        sems.at[step, layer, side],
                    )
                )
                copies[-1].start()
    return copies


def first_kernel(
    table_ref, near_ids_ref, far_ref, far_ids_ref, gate_ref, up_ref, gate_out, up_out,
    in_ref, base_ref, held_ref, in_sems, base_sems, sems,
):
    layers, rows, narrow = gate_ref.shape
    order = list(range(layers))[::-1]
    loads = load_weights(order, gate_ref, up_ref, in_ref, in_sems)
    scale = 1.0 / count_of(
        table_ref[...], iota((rows, 1), 0) + lax.axis_index("section") * rows
    )
    outs = (gate_out, up_out)
    copies = []
    for number, load in enumerate(loads):
        at, side = number // 2, number % 2
        load.wait()
        here = pl.ds(side * rows, rows)
        columns = in_ref[at, :, side * narrow : (side + 1) * narrow]
        base_ref[at, here] = (columns.astype(F32) * scale).astype(BF16)
        copies.append(
            pltpu.make_async_copy(
                base_ref.at[at, here],
                outs[side].at[order[at], 0, :, pl.ds(0, narrow)],
                base_sems.at[at, side],
            )
        )
        copies[-1].start()

    def near(start, size):
        return onehot_dot(base_ref.at[0], near_ids_ref[:, start : start + size], narrow)

    copies += put_extras(0, narrow, near, far_ref, far_ids_ref, outs, held_ref, sems)
    for copy in copies:
        copy.wait()


def first_half(table, near_ids, far, far_ids, gate, up, out_type):
    layers, rows, narrow = gate.shape
    extra = near_ids.shape[1]
    return pl.pallas_call(
        first_kernel,
        out_shape=(out_type, out_type),
        in_specs=[VMEM] * 4 + [HBM] * 2,
        out_specs=(HBM, HBM),
        scratch_shapes=[
            pltpu.VMEM((layers, rows, 2 * narrow), BF16),
            pltpu.VMEM((layers, 2 * rows, narrow), BF16),
            pltpu.VMEM((2 * rows, extra), BF16),
            pltpu.SemaphoreType.DMA((layers, 2)),
            pltpu.SemaphoreType.DMA((layers, 2)),
            pltpu.SemaphoreType.DMA((len(column_tiles(extra)), layers, 2)),
        ],
        compiler_params=PARAMS,
        cost_estimate=pl.CostEstimate(
            flops=4 * rows * (narrow + far.shape[2] * far.shape[0]) * extra,
            bytes_accessed=8 * layers * rows * (narrow + extra),
            transcendentals=0,
        ),
        name="first_half",
    )(table, near_ids, far, far_ids, gate, up)


def second_kernel(
    rows_ref, near_ref, far_ref, ids_ref, gate_in, up_in, gate_out, up_out,
    held_ref, base_sems, sems,
):
    rows, narrow = rows_ref.shape[0] // 2, rows_ref.shape[1]
    outs = (gate_out, up_out)
    layers = gate_out.shape[0]
    copies = []
    for side, out in enumerate(outs):
        copies.append(
            pltpu.make_async_copy(
                rows_ref.at[pl.ds(side * rows, rows), :],
                out.at[layers - 1, 1, :, pl.ds(0, narrow)],
                base_sems.at[side],
            )
        )
        copies[-1].start()

    def near(start, size):
        return near_ref[:, start : start + size].astype(F32)

    copies += put_extras(1, narrow, near, far_ref, ids_ref, outs, held_ref, sems)
    for copy in copies:
        copy.wait()


def second_half(rows, near, far, ids, gate_out, up_out):
    count, narrow = rows.shape
    extra = near.shape[1]
    layers = gate_out.shape[0]
    out_type = jax.ShapeDtypeStruct(gate_out.shape, BF16)
    return pl.pallas_call(
        second_kernel,
        out_shape=(out_type, out_type),
        in_specs=[VMEM] * 4 + [HBM] * 2,
        out_specs=(HBM, HBM),
        input_output_aliases={4: 0, 5: 1},
        scratch_shapes=[
            pltpu.VMEM((count, extra), BF16),
            pltpu.SemaphoreType.DMA((2,)),
            pltpu.SemaphoreType.DMA((len(column_tiles(extra)), layers, 2)),
        ],
        compiler_params=PARAMS,
        cost_estimate=pl.CostEstimate(
            flops=2 * count * far.shape[2] * far.shape[0] * extra,
            bytes_accessed=4 * count * (narrow + layers * extra),
            transcendentals=0,
        ),
        name="second_half",
    )(rows, near, far, ids, gate_out, up_out)


def last_kernel(
    land_ref, came_ref, gate_in, up_in, gate_out, up_out, in_ref, held_ref, in_sems, out_sems
):
    narrow = came_ref.shape[1] // 2
    steps = in_sems.shape[1]
    width = narrow // steps
    loads, stores = [], []
    for number in range(2 * steps):
        columns = pl.ds(number * width, width)
        loads.append(
            pltpu.make_async_copy(
                came_ref.at[:, columns],
                in_ref.at[:, columns],
                in_sems.at[number // steps, number % steps],
            )
        )
        loads[-1].start()
    for side, out in enumerate((gate_out, up_out)):
        for step in range(steps):
            at = side * narrow + step * width
            loads[side * steps + step].wait()
            held_ref[:, at : at + width] = jnp.dot(
                land_ref[...], in_ref[:, at : at + width], preferred_element_type=F32
            ).astype(BF16)
            stores.append(
                pltpu.make_async_copy(
                    held_ref.at[:, pl.ds(at, width)],
                    out.at[0, 1, :, pl.ds(step * width, width)],
                    out_sems.at[side, step],
                )
            )
            stores[-1].start()
    for store in stores:
        store.wait()


def last_rows(land, came, gate_out, up_out):
    rows, slots = land.shape
    narrow = came.shape[1] // 2
    steps = 2
    out_type = jax.ShapeDtypeStruct(gate_out.shape, BF16)
    return pl.pallas_call(
        last_kernel,
        out_shape=(out_type, out_type),
        in_specs=[VMEM] + [HBM] * 3,
        out_specs=(HBM, HBM),
        input_output_aliases={2: 0, 3: 1},
        scratch_shapes=[
            pltpu.VMEM((slots, 2 * narrow), BF16),
            pltpu.VMEM((rows, 2 * narrow), BF16),
            pltpu.SemaphoreType.DMA((2, steps)),
            pltpu.SemaphoreType.DMA((2, steps)),
        ],
        compiler_params=PARAMS,
        cost_estimate=pl.CostEstimate(
            flops=4 * rows * slots * narrow,
            bytes_accessed=8 * rows * narrow,
            transcendentals=0,
        ),
        name="last_rows",
    )(land, came, gate_out, up_out)


def turn_around(sent, splits):
    return jnp.stack(
        [
            lax.ppermute(sent[turn - 1], "mp", [(i, (i + turn) % splits) for i in range(splits)])
            for turn in range(1, splits)
        ]
    )


def tiled_local(gate_weight, up_weight, hidden_map, ffn_map):
    layers, rows, narrow = gate_weight.shape
    blocks = lax.axis_size("section")
    splits = lax.axis_size("mp")
    extra = ffn_map.shape[0] // splits
    cap = rows // blocks
    column_cap = extra // splits
    width = -(-column_cap // 128) * 128
    table = hidden_map.reshape(blocks, rows)
    out_type = jax.ShapeDtypeStruct((layers, 2, rows, narrow + extra), BF16)

    def swap_rows(sent):
        return lax.all_to_all(sent, "section", split_axis=0, concat_axis=0, tiled=True)

    def cross(sent, p):
        return lax.ppermute(sent, "section", [(i, i ^ p) for i in range(blocks)])

    sent_top = send_rows(table, gate_weight, up_weight, layers - 1, cap)
    came_top = [sent_top[0]] + [cross(sent_top[p], p) for p in range(1, blocks)]
    columns = ffn_map.reshape(-1, 128)
    own_sent, near_ids, send_ids, far_ids, sent_low = middle(
        table, columns, gate_weight, up_weight, cap, splits, width
    )
    own_far = turn_around(own_sent, splits)
    came_low = swap_rows(sent_low)
    land = land_rows(table, cap)
    got, got_sent = arrive_rows(land, send_ids, came_top)
    got_far = turn_around(got_sent, splits)
    outs = first_half(table, near_ids, own_far, far_ids, gate_weight, up_weight, out_type)
    got_near = near_columns(got, near_ids)
    outs = second_half(got, got_near, got_far, far_ids, *outs)
    return last_rows(land, came_low, *outs)


def plain_local(gate_weight, up_weight, hidden_map, ffn_map):
    layers, shard_rows, _ = gate_weight.shape
    blocks = lax.axis_size("section")
    splits = lax.axis_size("mp")
    section_rank = lax.axis_index("section")
    column_rank = lax.axis_index("mp")
    d_old = shard_rows * blocks
    extra_dev = ffn_map.shape[0] // splits
    route_cap = max(1, shard_rows // blocks)
    next_pick = jnp.minimum(jnp.arange(layers, dtype=jnp.int32) + 1, layers - 1) - 1
    counts = (
        jax.ops.segment_sum(jnp.ones((d_old,), jnp.float32), hidden_map, num_segments=d_old) + 1.0
    )
    own_rows = section_rank * shard_rows + jnp.arange(shard_rows, dtype=jnp.int32)
    copied = lax.dynamic_slice_in_dim(hidden_map, section_rank * shard_rows, shard_rows)
    mine_extra = lax.dynamic_slice_in_dim(ffn_map, column_rank * extra_dev, extra_dev)
    table = hidden_map.reshape(blocks, shard_rows)
    owner = table // shard_rows
    wanted = owner == section_rank
    order = jnp.cumsum(wanted.astype(jnp.int32), axis=1) - 1
    slot_ids = jnp.arange(route_cap, dtype=jnp.int32)
    selected = wanted[:, None, :] & (order[:, None, :] == slot_ids[None, :, None])
    sent_rows = jnp.sum(jnp.where(selected, (table % shard_rows)[:, None, :], 0), axis=2).reshape(
        -1
    )
    mine_owner = copied // shard_rows
    row_ids = jnp.arange(shard_rows, dtype=jnp.int32)
    earlier = row_ids[None, :] < row_ids[:, None]
    rank_among = jnp.sum(
        (earlier & (mine_owner[None, :] == mine_owner[:, None])).astype(jnp.int32), axis=1
    )
    landing = mine_owner * route_cap + rank_among
    pair = (gate_weight, up_weight)
    later = tuple((portion[1:] for portion in pair))
    rows_here = pair[0].shape[1]

    def pick_columns(carried, pieces):
        amount = pieces[0].shape[2]
        inside = (mine_extra >= 0) & (mine_extra < amount)
        bounded = jnp.clip(mine_extra, 0, amount - 1)
        return tuple(
            (
                jnp.where(inside, jnp.take(portion, bounded, axis=2), current)
                for current, portion in zip(carried, pieces)
            )
        )

    empty_extra = jnp.zeros((layers - 1, rows_here, extra_dev), jnp.bfloat16)
    extras = pick_columns(
        (empty_extra, empty_extra),
        (
            lax.all_gather(later[0], "mp", axis=2, tiled=True),
            lax.all_gather(later[1], "mp", axis=2, tiled=True),
        ),
    )
    own_gate, own_up = tuple(
        (
            jnp.concatenate([portion, added[next_pick]], axis=2)
            for portion, added in zip(pair, extras)
        )
    )
    arrived = (
        lax.all_to_all(
            jnp.take(own_gate, sent_rows, axis=1),
            "section",
            split_axis=1,
            concat_axis=1,
            tiled=True,
        ),
        lax.all_to_all(
            jnp.take(own_up, sent_rows, axis=1), "section", split_axis=1, concat_axis=1, tiled=True
        ),
    )
    grown_gate = jnp.stack([own_gate, jnp.take(arrived[0], landing, axis=1)], axis=1)
    grown_up = jnp.stack([own_up, jnp.take(arrived[1], landing, axis=1)], axis=1)
    divisor = jnp.stack([counts[own_rows], counts[copied]])[None, :, :, None]
    return (
        (grown_gate.astype(jnp.float32) / divisor).astype(jnp.bfloat16),
        (grown_up.astype(jnp.float32) / divisor).astype(jnp.bfloat16),
    )


def local(gate_weight, up_weight, hidden_map, ffn_map):
    layers, rows, narrow = gate_weight.shape
    blocks = lax.axis_size("section")
    splits = lax.axis_size("mp")
    extra = ffn_map.shape[0] // splits
    whole_tiles = (
        layers == 2
        and splits > 1
        and blocks > 1
        and blocks & (blocks - 1) == 0
        and rows % (8 * blocks) == 0
        and rows % 16 == 0
        and narrow % 256 == 0
        and extra % 128 == 0
        and extra % splits == 0
    )
    form = tiled_local if whole_tiles else plain_local
    return form(gate_weight, up_weight, hidden_map, ffn_map)


def solution(mesh):
    in_specs = (P(None, "section", "mp"), P(None, "section", "mp"), P(), P())
    out_specs = (P(None, None, "section", "mp"), P(None, None, "section", "mp"))
    return jax.shard_map(local, mesh=mesh, in_specs=in_specs, out_specs=out_specs, check_vma=False)
```

```python
import functools

import jax
import jax.numpy as jnp
from jax import lax
from jax.experimental import pallas as pl
from jax.experimental.pallas import tpu as pltpu
from jax.sharding import PartitionSpec as P


F32 = jnp.float32
BF16 = jnp.bfloat16
I32 = jnp.int32
VMEM = pl.BlockSpec(memory_space=pltpu.VMEM)
HBM = pl.BlockSpec(memory_space=pl.ANY)
K_CHUNK = 256
PARAMS = pltpu.CompilerParams(vmem_limit_bytes=32 << 20)


def iota(shape, axis):
    return lax.broadcasted_iota(I32, shape, axis)


def count_of(table, ids):
    total = jnp.zeros((ids.shape[0], table.shape[1]), F32)
    for block in range(table.shape[0]):
        total += jnp.where(table[block : block + 1, :] == ids, 1.0, 0.0)
    return 1.0 + jnp.sum(total, axis=1, keepdims=True)


def pick_matrix(table, me, cap, key_ref, within_ref, targets):
    blocks, rows = table.shape
    owner = lax.div(table, jnp.full_like(table, rows))
    within_ref[...] = table - owner * rows
    wanted = owner == me
    before = (iota((rows, rows), 0) < iota((rows, rows), 1)).astype(F32).astype(BF16)
    order = jnp.dot(wanted.astype(F32).astype(BF16), before, preferred_element_type=F32)
    key_ref[...] = jnp.where(wanted, order.astype(I32), -1)
    slot = iota((cap, rows), 0)
    parts = []
    for target in targets:
        line = pl.ds(target, 1)
        parts.append(jnp.where(key_ref[line, :] == slot, within_ref[line, :], 0).astype(F32))
    row_of = jnp.sum(jnp.concatenate(parts, axis=0), axis=1, keepdims=True).astype(I32)
    pick = (iota((blocks * cap, rows), 1) == row_of).astype(F32).astype(BF16)
    return pick, count_of(table, row_of + me * rows)


def land_matrix(mine, blocks, cap):
    rows = mine.shape[1]
    across, down = iota((rows, rows), 1), iota((rows, rows), 0)
    column = jnp.sum(
        jnp.where(across == down, mine, 0).astype(F32), axis=1, keepdims=True
    ).astype(I32)
    owner_row = lax.div(mine, jnp.full_like(mine, rows))
    owner = lax.div(column, jnp.full_like(column, rows))
    earlier = (across < down) & (owner == owner_row)
    rank = jnp.sum(jnp.where(earlier, 1.0, 0.0), axis=1, keepdims=True).astype(I32)
    return (iota((rows, blocks * cap), 1) == owner * cap + rank).astype(F32).astype(BF16)


def onehot_dot(left, index_row, extent):
    total = None
    for start in range(0, extent, K_CHUNK):
        size = min(K_CHUNK, extent - start)
        mask = iota((size, index_row.shape[1]), 0) == index_row - start
        term = jnp.dot(
            left[:, start : start + size],
            mask.astype(F32).astype(BF16),
            preferred_element_type=F32,
        )
        total = term if total is None else total + term
    return total


def load_weights(layers, gate_ref, up_ref, in_ref, sems):
    narrow = gate_ref.shape[2]
    loads = []
    for at, layer in enumerate(layers):
        for side, ref in enumerate((gate_ref, up_ref)):
            loads.append(
                pltpu.make_async_copy(
                    ref.at[layer],
                    in_ref.at[at, :, pl.ds(side * narrow, narrow)],
                    sems.at[at, side],
                )
            )
            loads[-1].start()
    return loads


def put_slots(loads, pick, scale, in_ref, held_ref, sent_refs, sems):
    width = held_ref.shape[1] // len(loads)
    stores = []
    for side, load in enumerate(loads):
        columns = pl.ds(side * width, width)
        load.wait()
        rows = jnp.dot(pick, in_ref[:, columns], preferred_element_type=F32)
        held_ref[:, columns] = (rows * scale).astype(BF16)
        first = 0
        for piece, ref in enumerate(sent_refs):
            count = ref.shape[0]
            stores.append(
                pltpu.make_async_copy(
                    held_ref.at[pl.ds(first, count), columns],
                    ref.at[:, columns],
                    sems.at[side, piece],
                )
            )
            stores[-1].start()
            first += count
    return stores


def send_kernel(layer, cap, table_ref, gate_ref, up_ref, *refs):
    *sent_refs, map_ref, in_ref, held_ref, key_ref, within_ref, map_sem, in_sems, out_sems = refs
    map_load = pltpu.make_async_copy(table_ref, map_ref, map_sem)
    map_load.start()
    loads = load_weights([layer], gate_ref, up_ref, in_ref, in_sems)
    me = lax.axis_index("section")
    targets = [me ^ p for p in range(map_ref.shape[0])]
    map_load.wait()
    pick, count = pick_matrix(map_ref[...], me, cap, key_ref, within_ref, targets)
    stores = put_slots(loads, pick, 1.0 / count, in_ref.at[0], held_ref, sent_refs, out_sems)
    for store in stores:
        store.wait()


def send_rows(table, gate, up, layer, cap):
    _, rows, narrow = gate.shape
    blocks = table.shape[0]
    return pl.pallas_call(
        functools.partial(send_kernel, layer, cap),
        out_shape=[jax.ShapeDtypeStruct((cap, 2 * narrow), BF16)] * blocks,
        in_specs=[HBM] * 3,
        out_specs=[HBM] * blocks,
        scratch_shapes=[
            pltpu.VMEM((blocks, rows), I32),
            pltpu.VMEM((1, rows, 2 * narrow), BF16),
            pltpu.VMEM((blocks * cap, 2 * narrow), BF16),
            pltpu.VMEM((blocks, rows), I32),
            pltpu.VMEM((blocks, rows), I32),
            pltpu.SemaphoreType.DMA(()),
            pltpu.SemaphoreType.DMA((1, 2)),
            pltpu.SemaphoreType.DMA((2, blocks)),
        ],
        cost_estimate=pl.CostEstimate(
            flops=4 * blocks * cap * rows * narrow,
            bytes_accessed=8 * rows * narrow,
            transcendentals=0,
        ),
        name="send_rows",
    )(table, gate, up)


def running_order(hit):
    lines, lanes = hit.shape
    ones = hit.astype(F32)
    before = (iota((lanes, lanes), 0) < iota((lanes, lanes), 1)).astype(F32).astype(BF16)
    above = (iota((lines, lines), 1) < iota((lines, lines), 0)).astype(F32).astype(BF16)
    count = jnp.sum(ones, axis=1, keepdims=True)
    ahead = jnp.dot(
        above, jnp.broadcast_to(count, (lines, lanes)).astype(BF16), preferred_element_type=F32
    )[:, :1]
    inside = jnp.dot(ones.astype(BF16), before, preferred_element_type=F32)
    return jnp.where(hit, inside, -1.0), ahead, count


def slot_columns(inside, ahead, count, within, width):
    lines, _ = inside.shape
    slot = iota((lines, width), 1).astype(F32)
    chosen = (slot >= ahead) & (slot < ahead + count)
    spread = chosen.astype(F32).astype(BF16)
    first = jnp.sum(jnp.where(chosen, ahead, 0.0), axis=0, keepdims=True)
    used = jnp.sum(chosen.astype(F32), axis=0, keepdims=True)
    high = lax.div(within, jnp.full_like(within, 256))
    low = within - high * 256

    def over_slots(value):
        return lax.dot_general(
            value.astype(F32).astype(BF16),
            spread,
            (((0,), (0,)), ((), ())),
            preferred_element_type=F32,
        )

    order = slot[:1] - first
    hit = over_slots(inside) == order
    column = jnp.sum(
        jnp.where(hit, over_slots(high) * 256.0 + over_slots(low), 0.0), axis=0, keepdims=True
    )
    return jnp.where(used > 0.0, column, -1.0).astype(I32)


def column_plan(narrow, map_ref, near_ref, send_ref, far_ref, splits):
    rank = lax.axis_index("mp")
    lines = map_ref.shape[0] // splits
    lanes = map_ref.shape[1]
    blocks = [map_ref[split * lines : (split + 1) * lines, :] for split in range(splits)]

    def block_of(index):
        chosen = blocks[0]
        for split in range(1, splits):
            chosen = jnp.where(index == split, blocks[split], chosen)
        owner = lax.div(chosen, jnp.full_like(chosen, narrow))
        return owner, chosen - owner * narrow

    def flatten(value, ref, at):
        for line in range(lines):
            ref[at : at + 1, line * lanes : (line + 1) * lanes] = value[line : line + 1, :]

    owner, within = block_of(rank)
    flatten(jnp.where(owner == rank, within, -1), near_ref, 0)
    for turn in range(1, splits):
        hit = owner == lax.rem(rank + splits - turn, splits)
        inside, ahead, _ = running_order(hit)
        flatten(jnp.where(hit, inside + ahead, -1.0).astype(I32), far_ref, turn - 1)
        their_owner, their_within = block_of(lax.rem(rank + turn, splits))
        inside, ahead, count = running_order(their_owner == rank)
        send_ref[turn - 1 : turn, :] = slot_columns(
            inside, ahead, count, their_within, send_ref.shape[1]
        )


def middle_kernel(
    cap, splits, table_ref, map_ref, gate_ref, up_ref, turn_ref, near_ref, send_ref, far_ref, sent_ref,
    in_ref, own_ref, held_ref, key_ref, within_ref, in_sems, out_sems,
):
    layers, rows, narrow = gate_ref.shape
    loads = load_weights([layers - 1, 0], gate_ref, up_ref, in_ref, in_sems)
    me = lax.axis_index("section")
    table = table_ref[...]
    column_plan(narrow, map_ref, near_ref, send_ref, far_ref, splits)
    scale = 1.0 / count_of(table, iota((rows, 1), 0) + me * rows)
    pick, count = pick_matrix(table, me, cap, key_ref, within_ref, list(range(table.shape[0])))
    stores = put_slots(
        loads[2:], pick, 1.0 / count, in_ref.at[1], held_ref, (sent_ref,), out_sems
    )
    for side, load in enumerate(loads[:2]):
        load.wait()
        columns = in_ref[0, :, side * narrow : (side + 1) * narrow]
        own_ref[side * rows : (side + 1) * rows] = (columns.astype(F32) * scale).astype(BF16)
    for s in range(splits - 1):
        turn_ref[s] = onehot_dot(own_ref, send_ref[s : s + 1, :], narrow).astype(BF16)
    for store in stores:
        store.wait()


def middle(table, columns, gate, up, cap, splits, width):
    _, rows, narrow = gate.shape
    blocks = table.shape[0]
    extra = columns.size // splits
    return pl.pallas_call(
        functools.partial(middle_kernel, cap, splits),
        out_shape=(
            jax.ShapeDtypeStruct((splits - 1, 2 * rows, width), BF16),
            jax.ShapeDtypeStruct((1, extra), I32),
            jax.ShapeDtypeStruct((splits - 1, width), I32),
            jax.ShapeDtypeStruct((splits - 1, extra), I32),
            jax.ShapeDtypeStruct((blocks * cap, 2 * narrow), BF16),
        ),
        in_specs=[VMEM, VMEM, HBM, HBM],
        out_specs=(VMEM, VMEM, VMEM, VMEM, HBM),
        scratch_shapes=[
            pltpu.VMEM((2, rows, 2 * narrow), BF16),
            pltpu.VMEM((2 * rows, narrow), BF16),
            pltpu.VMEM((blocks * cap, 2 * narrow), BF16),
            pltpu.VMEM((blocks, rows), I32),
            pltpu.VMEM((blocks, rows), I32),
            pltpu.SemaphoreType.DMA((2, 2)),
            pltpu.SemaphoreType.DMA((2, 1)),
        ],
        cost_estimate=pl.CostEstimate(
            flops=4 * rows * narrow * width,
            bytes_accessed=16 * rows * narrow,
            transcendentals=0,
        ),
        name="middle",
    )(table, columns, gate, up)


def land_kernel(cap, table_ref, land_ref):
    mine = table_ref[pl.ds(lax.axis_index("section"), 1), :]
    land_ref[...] = land_matrix(mine, table_ref.shape[0], cap)


def land_rows(table, cap):
    blocks, rows = table.shape
    return pl.pallas_call(
        functools.partial(land_kernel, cap),
        out_shape=jax.ShapeDtypeStruct((rows, blocks * cap), BF16),
        in_specs=[VMEM],
        out_specs=VMEM,
        compiler_params=PARAMS,
        name="land_rows",
    )(table)


def arrive_kernel(land_ref, ids_ref, *refs):
    *came_refs, rows_ref, gate_ref, up_ref, held_ref, sems = refs
    narrow = rows_ref.shape[1]
    rows = land_ref.shape[0]
    cap = came_refs[0].shape[0]
    me = lax.axis_index("section")
    starts = [me ^ p for p in range(len(came_refs))]
    loads = []
    for piece, (ref, start) in enumerate(zip(came_refs, starts)):
        where = pl.ds(pl.multiple_of(start * cap, cap), ref.shape[0])
        loads.append(pltpu.make_async_copy(ref, held_ref.at[where, :], sems.at[piece]))
        loads[-1].start()
    for load in loads:
        load.wait()
    for side in range(2):
        rows_ref[side * rows : (side + 1) * rows] = jnp.dot(
            land_ref[...],
            held_ref[:, side * narrow : (side + 1) * narrow],
            preferred_element_type=F32,
        ).astype(BF16)
    for s in range(ids_ref.shape[0]):
        picked = onehot_dot(rows_ref, ids_ref[s : s + 1, :], narrow).astype(BF16)
        gate_ref[s] = picked[:rows]
        up_ref[s] = picked[rows:]


def arrive_rows(land, ids, came):
    rows, slots = land.shape
    narrow = came[0].shape[1] // 2
    turns, width = ids.shape
    return pl.pallas_call(
        arrive_kernel,
        out_shape=(
            jax.ShapeDtypeStruct((2 * rows, narrow), BF16),
            jax.ShapeDtypeStruct((turns, rows, width), BF16),
            jax.ShapeDtypeStruct((turns, rows, width), BF16),
        ),
        in_specs=[VMEM, VMEM] + [HBM] * len(came),
        out_specs=(VMEM,) * 3,
        scratch_shapes=[
            pltpu.VMEM((slots, 2 * narrow), BF16),
            pltpu.SemaphoreType.DMA((len(came),)),
        ],
        compiler_params=PARAMS,
        cost_estimate=pl.CostEstimate(
            flops=4 * rows * narrow * width * turns,
            bytes_accessed=8 * rows * narrow,
            transcendentals=0,
        ),
        name="arrive_rows",
    )(land, ids, *came)


def near_kernel(rows_ref, ids_ref, out_ref):
    for start, size in column_tiles(ids_ref.shape[1]):
        out_ref[:, start : start + size] = onehot_dot(
            rows_ref, ids_ref[:, start : start + size], rows_ref.shape[1]
        ).astype(BF16)


def near_columns(rows, ids):
    count, narrow = rows.shape
    extra = ids.shape[1]
    return pl.pallas_call(
        near_kernel,
        out_shape=jax.ShapeDtypeStruct((count, extra), BF16),
        in_specs=[VMEM] * 2,
        out_specs=VMEM,
        compiler_params=PARAMS,
        cost_estimate=pl.CostEstimate(
            flops=2 * count * narrow * extra,
            bytes_accessed=2 * count * (narrow + extra),
            transcendentals=0,
        ),
    )(rows, ids)


def column_tiles(extent):
    pieces = -(-extent // 1408)
    size = extent // pieces // 256 * 256 or extent
    starts = [size * piece for piece in range(pieces)]
    return [
        (start, (extent if start == starts[-1] else start + size) - start) for start in starts
    ]


def put_extras(half, narrow, near, far_ref, ids_ref, outs, held_ref, sems):
    rows = held_ref.shape[0] // len(outs)
    layers = outs[0].shape[0]
    copies = []
    for step, (start, size) in enumerate(column_tiles(held_ref.shape[1])):
        total = None
        for s in range(ids_ref.shape[0]):
            far = onehot_dot(far_ref.at[s], ids_ref[s : s + 1, start : start + size], far_ref.shape[2])
            total = far if total is None else total + far
        held_ref[:, start : start + size] = (total + near(start, size)).astype(BF16)
        for layer in range(layers):
            for side, out in enumerate(outs):
                copies.append(
                    pltpu.make_async_copy(
                        held_ref.at[pl.ds(side * rows, rows), pl.ds(start, size)],
                        out.at[layer, half, :, pl.ds(narrow + start, size)],
                        sems.at[step, layer, side],
                    )
                )
                copies[-1].start()
    return copies


def first_kernel(
    table_ref, near_ids_ref, far_ref, far_ids_ref, gate_ref, up_ref, gate_out, up_out,
    in_ref, base_ref, held_ref, in_sems, base_sems, sems,
):
    layers, rows, narrow = gate_ref.shape
    order = list(range(layers))[::-1]
    loads = load_weights(order, gate_ref, up_ref, in_ref, in_sems)
    scale = 1.0 / count_of(
        table_ref[...], iota((rows, 1), 0) + lax.axis_index("section") * rows
    )
    outs = (gate_out, up_out)
    copies = []
    for number, load in enumerate(loads):
        at, side = number // 2, number % 2
        load.wait()
        here = pl.ds(side * rows, rows)
        columns = in_ref[at, :, side * narrow : (side + 1) * narrow]
        base_ref[at, here] = (columns.astype(F32) * scale).astype(BF16)
        copies.append(
            pltpu.make_async_copy(
                base_ref.at[at, here],
                outs[side].at[order[at], 0, :, pl.ds(0, narrow)],
                base_sems.at[at, side],
            )
        )
        copies[-1].start()

    def near(start, size):
        return onehot_dot(base_ref.at[0], near_ids_ref[:, start : start + size], narrow)

    copies += put_extras(0, narrow, near, far_ref, far_ids_ref, outs, held_ref, sems)
    for copy in copies:
        copy.wait()


def first_half(table, near_ids, far, far_ids, gate, up, out_type):
    layers, rows, narrow = gate.shape
    extra = near_ids.shape[1]
    return pl.pallas_call(
        first_kernel,
        out_shape=(out_type, out_type),
        in_specs=[VMEM] * 4 + [HBM] * 2,
        out_specs=(HBM, HBM),
        scratch_shapes=[
            pltpu.VMEM((layers, rows, 2 * narrow), BF16),
            pltpu.VMEM((layers, 2 * rows, narrow), BF16),
            pltpu.VMEM((2 * rows, extra), BF16),
            pltpu.SemaphoreType.DMA((layers, 2)),
            pltpu.SemaphoreType.DMA((layers, 2)),
            pltpu.SemaphoreType.DMA((len(column_tiles(extra)), layers, 2)),
        ],
        compiler_params=PARAMS,
        cost_estimate=pl.CostEstimate(
            flops=4 * rows * (narrow + far.shape[2] * far.shape[0]) * extra,
            bytes_accessed=8 * layers * rows * (narrow + extra),
            transcendentals=0,
        ),
        name="first_half",
    )(table, near_ids, far, far_ids, gate, up)


def second_kernel(
    rows_ref, near_ref, far_ref, ids_ref, old_ref, out_ref, held_ref, base_sem, sems
):
    narrow = rows_ref.shape[1]
    layers = out_ref.shape[0]
    copies = [
        pltpu.make_async_copy(rows_ref, out_ref.at[layers - 1, 1, :, pl.ds(0, narrow)], base_sem)
    ]
    copies[0].start()

    def near(start, size):
        return near_ref[:, start : start + size].astype(F32)

    copies += put_extras(1, narrow, near, far_ref, ids_ref, (out_ref,), held_ref, sems)
    for copy in copies:
        copy.wait()


def second_half(rows, near, far, ids, out, side):
    count, narrow = rows.shape[0] // 2, rows.shape[1]
    extra = near.shape[1]
    layers = out.shape[0]
    return pl.pallas_call(
        second_kernel,
        out_shape=jax.ShapeDtypeStruct(out.shape, BF16),
        grid=(1,),
        in_specs=[
            pl.BlockSpec((count, narrow), lambda i: (side, 0)),
            pl.BlockSpec((count, extra), lambda i: (side, 0)),
            pl.BlockSpec(far.shape, lambda i: (0, 0, 0)),
            pl.BlockSpec(ids.shape, lambda i: (0, 0)),
            HBM,
        ],
        out_specs=HBM,
        input_output_aliases={4: 0},
        scratch_shapes=[
            pltpu.VMEM((count, extra), BF16),
            pltpu.SemaphoreType.DMA(()),
            pltpu.SemaphoreType.DMA((len(column_tiles(extra)), layers, 1)),
        ],
        compiler_params=PARAMS,
        cost_estimate=pl.CostEstimate(
            flops=2 * count * far.shape[2] * far.shape[0] * extra,
            bytes_accessed=4 * count * (narrow + layers * extra),
            transcendentals=0,
        ),
    )(rows, near, far, ids, out)


def last_kernel(land_ref, came_ref, gate_in, up_in, gate_out, up_out, held_ref, sems):
    narrow = came_ref.shape[1] // 2
    steps = sems.shape[1]
    width = narrow // steps
    stores = []
    for side, out in enumerate((gate_out, up_out)):
        for step in range(steps):
            at = side * narrow + step * width
            held_ref[:, at : at + width] = jnp.dot(
                land_ref[...], came_ref[:, at : at + width], preferred_element_type=F32
            ).astype(BF16)
            stores.append(
                pltpu.make_async_copy(
                    held_ref.at[:, pl.ds(at, width)],
                    out.at[0, 1, :, pl.ds(step * width, width)],
                    sems.at[side, step],
                )
            )
            stores[-1].start()
    for store in stores:
        store.wait()


def last_rows(land, came, gate_out, up_out):
    rows, slots = land.shape
    narrow = came.shape[1] // 2
    steps = 2
    out_type = jax.ShapeDtypeStruct(gate_out.shape, BF16)
    return pl.pallas_call(
        last_kernel,
        out_shape=(out_type, out_type),
        in_specs=[VMEM] * 2 + [HBM] * 2,
        out_specs=(HBM, HBM),
        input_output_aliases={2: 0, 3: 1},
        scratch_shapes=[
            pltpu.VMEM((rows, 2 * narrow), BF16),
            pltpu.SemaphoreType.DMA((2, steps)),
        ],
        compiler_params=PARAMS,
        cost_estimate=pl.CostEstimate(
            flops=4 * rows * slots * narrow,
            bytes_accessed=8 * rows * narrow,
            transcendentals=0,
        ),
        name="last_rows",
    )(land, came, gate_out, up_out)


def turn_around(sent, splits):
    return jnp.stack(
        [
            lax.ppermute(sent[turn - 1], "mp", [(i, (i + turn) % splits) for i in range(splits)])
            for turn in range(1, splits)
        ]
    )


def tiled_local(gate_weight, up_weight, hidden_map, ffn_map):
    layers, rows, narrow = gate_weight.shape
    blocks = lax.axis_size("section")
    splits = lax.axis_size("mp")
    extra = ffn_map.shape[0] // splits
    cap = rows // blocks
    column_cap = extra // splits
    width = -(-column_cap // 128) * 128
    table = hidden_map.reshape(blocks, rows)
    out_type = jax.ShapeDtypeStruct((layers, 2, rows, narrow + extra), BF16)

    def swap_rows(sent):
        return lax.all_to_all(sent, "section", split_axis=0, concat_axis=0, tiled=True)

    def cross(sent, p):
        return lax.ppermute(sent, "section", [(i, i ^ p) for i in range(blocks)])

    sent_top = send_rows(table, gate_weight, up_weight, layers - 1, cap)
    came_top = [sent_top[0]] + [cross(sent_top[p], p) for p in range(1, blocks)]
    columns = ffn_map.reshape(-1, 128)
    own_sent, near_ids, send_ids, far_ids, sent_low = middle(
        table, columns, gate_weight, up_weight, cap, splits, width
    )
    own_far = turn_around(own_sent, splits)
    came_low = swap_rows(sent_low)
    land = land_rows(table, cap)
    got, *got_sent = arrive_rows(land, send_ids, came_top)
    got_far = [turn_around(got_sent[side], splits) for side in range(2)]
    outs = first_half(table, near_ids, own_far, far_ids, gate_weight, up_weight, out_type)
    got_near = near_columns(got, near_ids)
    outs = [
        second_half(got, got_near, got_far[side], far_ids, outs[side], side)
        for side in range(2)
    ]
    return last_rows(land, came_low, *outs)


def plain_local(gate_weight, up_weight, hidden_map, ffn_map):
    layers, shard_rows, _ = gate_weight.shape
    blocks = lax.axis_size("section")
    splits = lax.axis_size("mp")
    section_rank = lax.axis_index("section")
    column_rank = lax.axis_index("mp")
    d_old = shard_rows * blocks
    extra_dev = ffn_map.shape[0] // splits
    route_cap = max(1, shard_rows // blocks)
    next_pick = jnp.minimum(jnp.arange(layers, dtype=jnp.int32) + 1, layers - 1) - 1
    counts = (
        jax.ops.segment_sum(jnp.ones((d_old,), jnp.float32), hidden_map, num_segments=d_old) + 1.0
    )
    own_rows = section_rank * shard_rows + jnp.arange(shard_rows, dtype=jnp.int32)
    copied = lax.dynamic_slice_in_dim(hidden_map, section_rank * shard_rows, shard_rows)
    mine_extra = lax.dynamic_slice_in_dim(ffn_map, column_rank * extra_dev, extra_dev)
    table = hidden_map.reshape(blocks, shard_rows)
    owner = table // shard_rows
    wanted = owner == section_rank
    order = jnp.cumsum(wanted.astype(jnp.int32), axis=1) - 1
    slot_ids = jnp.arange(route_cap, dtype=jnp.int32)
    selected = wanted[:, None, :] & (order[:, None, :] == slot_ids[None, :, None])
    sent_rows = jnp.sum(jnp.where(selected, (table % shard_rows)[:, None, :], 0), axis=2).reshape(
        -1
    )
    mine_owner = copied // shard_rows
    row_ids = jnp.arange(shard_rows, dtype=jnp.int32)
    earlier = row_ids[None, :] < row_ids[:, None]
    rank_among = jnp.sum(
        (earlier & (mine_owner[None, :] == mine_owner[:, None])).astype(jnp.int32), axis=1
    )
    landing = mine_owner * route_cap + rank_among
    pair = (gate_weight, up_weight)
    later = tuple((portion[1:] for portion in pair))
    rows_here = pair[0].shape[1]

    def pick_columns(carried, pieces):
        amount = pieces[0].shape[2]
        inside = (mine_extra >= 0) & (mine_extra < amount)
        bounded = jnp.clip(mine_extra, 0, amount - 1)
        return tuple(
            (
                jnp.where(inside, jnp.take(portion, bounded, axis=2), current)
                for current, portion in zip(carried, pieces)
            )
        )

    empty_extra = jnp.zeros((layers - 1, rows_here, extra_dev), jnp.bfloat16)
    extras = pick_columns(
        (empty_extra, empty_extra),
        (
            lax.all_gather(later[0], "mp", axis=2, tiled=True),
            lax.all_gather(later[1], "mp", axis=2, tiled=True),
        ),
    )
    own_gate, own_up = tuple(
        (
            jnp.concatenate([portion, added[next_pick]], axis=2)
            for portion, added in zip(pair, extras)
        )
    )
    arrived = (
        lax.all_to_all(
            jnp.take(own_gate, sent_rows, axis=1),
            "section",
            split_axis=1,
            concat_axis=1,
            tiled=True,
        ),
        lax.all_to_all(
            jnp.take(own_up, sent_rows, axis=1), "section", split_axis=1, concat_axis=1, tiled=True
        ),
    )
    grown_gate = jnp.stack([own_gate, jnp.take(arrived[0], landing, axis=1)], axis=1)
    grown_up = jnp.stack([own_up, jnp.take(arrived[1], landing, axis=1)], axis=1)
    divisor = jnp.stack([counts[own_rows], counts[copied]])[None, :, :, None]
    return (
        (grown_gate.astype(jnp.float32) / divisor).astype(jnp.bfloat16),
        (grown_up.astype(jnp.float32) / divisor).astype(jnp.bfloat16),
    )


def local(gate_weight, up_weight, hidden_map, ffn_map):
    layers, rows, narrow = gate_weight.shape
    blocks = lax.axis_size("section")
    splits = lax.axis_size("mp")
    extra = ffn_map.shape[0] // splits
    whole_tiles = (
        layers == 2
        and splits > 1
        and blocks > 1
        and blocks & (blocks - 1) == 0
        and rows % (8 * blocks) == 0
        and rows % 16 == 0
        and narrow % 256 == 0
        and extra % 128 == 0
        and extra % splits == 0
    )
    form = tiled_local if whole_tiles else plain_local
    return form(gate_weight, up_weight, hidden_map, ffn_map)


def solution(mesh):
    in_specs = (P(None, "section", "mp"), P(None, "section", "mp"), P(), P())
    out_specs = (P(None, None, "section", "mp"), P(None, None, "section", "mp"))
    return jax.shard_map(local, mesh=mesh, in_specs=in_specs, out_specs=out_specs, check_vma=False)
```

```python
import functools

import jax
import jax.numpy as jnp
from jax import lax
from jax.experimental import pallas as pl
from jax.experimental.pallas import tpu as pltpu
from jax.sharding import PartitionSpec as P


F32 = jnp.float32
BF16 = jnp.bfloat16
I32 = jnp.int32
VMEM = pl.BlockSpec(memory_space=pltpu.VMEM)
HBM = pl.BlockSpec(memory_space=pl.ANY)
K_CHUNK = 256
MOVED_TILES = 2
PARAMS = pltpu.CompilerParams(vmem_limit_bytes=32 << 20)


def iota(shape, axis):
    return lax.broadcasted_iota(I32, shape, axis)


def count_of(table, ids):
    total = jnp.zeros((ids.shape[0], table.shape[1]), F32)
    for block in range(table.shape[0]):
        total += jnp.where(table[block : block + 1, :] == ids, 1.0, 0.0)
    return 1.0 + jnp.sum(total, axis=1, keepdims=True)


def pick_matrix(table, me, cap, key_ref, within_ref, targets):
    blocks, rows = table.shape
    owner = lax.div(table, jnp.full_like(table, rows))
    within_ref[...] = table - owner * rows
    wanted = owner == me
    before = (iota((rows, rows), 0) < iota((rows, rows), 1)).astype(F32).astype(BF16)
    order = jnp.dot(wanted.astype(F32).astype(BF16), before, preferred_element_type=F32)
    key_ref[...] = jnp.where(wanted, order.astype(I32), -1)
    slot = iota((cap, rows), 0)
    parts = []
    for target in targets:
        line = pl.ds(target, 1)
        parts.append(jnp.where(key_ref[line, :] == slot, within_ref[line, :], 0).astype(F32))
    row_of = jnp.sum(jnp.concatenate(parts, axis=0), axis=1, keepdims=True).astype(I32)
    pick = (iota((blocks * cap, rows), 1) == row_of).astype(F32).astype(BF16)
    return pick, count_of(table, row_of + me * rows)


def land_matrix(mine, blocks, cap):
    rows = mine.shape[1]
    across, down = iota((rows, rows), 1), iota((rows, rows), 0)
    column = jnp.sum(
        jnp.where(across == down, mine, 0).astype(F32), axis=1, keepdims=True
    ).astype(I32)
    owner_row = lax.div(mine, jnp.full_like(mine, rows))
    owner = lax.div(column, jnp.full_like(column, rows))
    earlier = (across < down) & (owner == owner_row)
    rank = jnp.sum(jnp.where(earlier, 1.0, 0.0), axis=1, keepdims=True).astype(I32)
    return (iota((rows, blocks * cap), 1) == owner * cap + rank).astype(F32).astype(BF16)


def onehot_dot(left, index_row, extent):
    total = None
    for start in range(0, extent, K_CHUNK):
        size = min(K_CHUNK, extent - start)
        mask = iota((size, index_row.shape[1]), 0) == index_row - start
        term = jnp.dot(
            left[:, start : start + size],
            mask.astype(F32).astype(BF16),
            preferred_element_type=F32,
        )
        total = term if total is None else total + term
    return total


def load_weights(layers, gate_ref, up_ref, in_ref, sems):
    narrow = gate_ref.shape[2]
    loads = []
    for at, layer in enumerate(layers):
        for side, ref in enumerate((gate_ref, up_ref)):
            loads.append(
                pltpu.make_async_copy(
                    ref.at[layer],
                    in_ref.at[at, :, pl.ds(side * narrow, narrow)],
                    sems.at[at, side],
                )
            )
            loads[-1].start()
    return loads


def put_slots(parts, pick, scale, held_ref, sent_refs, sems):
    stores = []
    for number, (load, source, start) in enumerate(parts):
        columns = pl.ds(start, source.shape[1])
        load.wait()
        rows = jnp.dot(pick, source[...], preferred_element_type=F32)
        held_ref[:, columns] = (rows * scale).astype(BF16)
        first = 0
        for piece, ref in enumerate(sent_refs):
            count = ref.shape[0]
            stores.append(
                pltpu.make_async_copy(
                    held_ref.at[pl.ds(first, count), columns],
                    ref.at[:, columns],
                    sems.at[number, piece],
                )
            )
            stores[-1].start()
            first += count
    return stores


def send_kernel(layer, cap, table_ref, gate_ref, up_ref, *refs):
    *sent_refs, map_ref, in_ref, rest_ref, held_ref, key_ref, within_ref = refs[:-4]
    map_sem, in_sems, rest_sem, out_sems = refs[-4:]
    narrow, moved = gate_ref.shape[2], rest_ref.shape[1]
    map_load = pltpu.make_async_copy(table_ref, map_ref, map_sem)
    map_load.start()
    loads = load_weights([layer], gate_ref, up_ref, in_ref, in_sems)
    rest = pltpu.make_async_copy(up_ref.at[0, :, pl.ds(narrow - moved, moved)], rest_ref, rest_sem)
    rest.start()
    me = lax.axis_index("section")
    targets = [me ^ p for p in range(map_ref.shape[0])]
    map_load.wait()
    pick, count = pick_matrix(map_ref[...], me, cap, key_ref, within_ref, targets)
    parts = [
        (loads[0], in_ref.at[0, :, pl.ds(0, narrow)], 0),
        (loads[1], in_ref.at[0, :, pl.ds(narrow, narrow)], narrow),
        (rest, rest_ref, 2 * narrow),
    ]
    for store in put_slots(parts, pick, 1.0 / count, held_ref, sent_refs, out_sems):
        store.wait()


def send_rows(table, gate, up, layer, cap, moved):
    _, rows, narrow = gate.shape
    blocks = table.shape[0]
    return pl.pallas_call(
        functools.partial(send_kernel, layer, cap),
        out_shape=[jax.ShapeDtypeStruct((cap, 2 * narrow + moved), BF16)] * blocks,
        in_specs=[HBM] * 3,
        out_specs=[HBM] * blocks,
        scratch_shapes=[
            pltpu.VMEM((blocks, rows), I32),
            pltpu.VMEM((1, rows, 2 * narrow), BF16),
            pltpu.VMEM((rows, moved), BF16),
            pltpu.VMEM((blocks * cap, 2 * narrow + moved), BF16),
            pltpu.VMEM((blocks, rows), I32),
            pltpu.VMEM((blocks, rows), I32),
            pltpu.SemaphoreType.DMA(()),
            pltpu.SemaphoreType.DMA((1, 2)),
            pltpu.SemaphoreType.DMA(()),
            pltpu.SemaphoreType.DMA((3, blocks)),
        ],
        cost_estimate=pl.CostEstimate(
            flops=4 * blocks * cap * rows * narrow,
            bytes_accessed=8 * rows * narrow,
            transcendentals=0,
        ),
        name="send_rows",
    )(table, gate, up)


def running_order(hit):
    lines, lanes = hit.shape
    ones = hit.astype(F32)
    before = (iota((lanes, lanes), 0) < iota((lanes, lanes), 1)).astype(F32).astype(BF16)
    above = (iota((lines, lines), 1) < iota((lines, lines), 0)).astype(F32).astype(BF16)
    count = jnp.sum(ones, axis=1, keepdims=True)
    ahead = jnp.dot(
        above, jnp.broadcast_to(count, (lines, lanes)).astype(BF16), preferred_element_type=F32
    )[:, :1]
    inside = jnp.dot(ones.astype(BF16), before, preferred_element_type=F32)
    return jnp.where(hit, inside, -1.0), ahead, count


def slot_columns(inside, ahead, count, within, width):
    lines, _ = inside.shape
    slot = iota((lines, width), 1).astype(F32)
    chosen = (slot >= ahead) & (slot < ahead + count)
    spread = chosen.astype(F32).astype(BF16)
    first = jnp.sum(jnp.where(chosen, ahead, 0.0), axis=0, keepdims=True)
    used = jnp.sum(chosen.astype(F32), axis=0, keepdims=True)
    high = lax.div(within, jnp.full_like(within, 256))
    low = within - high * 256

    def over_slots(value):
        return lax.dot_general(
            value.astype(F32).astype(BF16),
            spread,
            (((0,), (0,)), ((), ())),
            preferred_element_type=F32,
        )

    order = slot[:1] - first
    hit = over_slots(inside) == order
    column = jnp.sum(
        jnp.where(hit, over_slots(high) * 256.0 + over_slots(low), 0.0), axis=0, keepdims=True
    )
    return jnp.where(used > 0.0, column, -1.0).astype(I32)


def column_plan(narrow, map_ref, near_ref, send_ref, far_ref, splits):
    rank = lax.axis_index("mp")
    lines = map_ref.shape[0] // splits
    lanes = map_ref.shape[1]
    blocks = [map_ref[split * lines : (split + 1) * lines, :] for split in range(splits)]

    def block_of(index):
        chosen = blocks[0]
        for split in range(1, splits):
            chosen = jnp.where(index == split, blocks[split], chosen)
        owner = lax.div(chosen, jnp.full_like(chosen, narrow))
        return owner, chosen - owner * narrow

    def flatten(value, ref, at):
        for line in range(lines):
            ref[at : at + 1, line * lanes : (line + 1) * lanes] = value[line : line + 1, :]

    owner, within = block_of(rank)
    flatten(jnp.where(owner == rank, within, -1), near_ref, 0)
    for turn in range(1, splits):
        hit = owner == lax.rem(rank + splits - turn, splits)
        inside, ahead, _ = running_order(hit)
        flatten(jnp.where(hit, inside + ahead, -1.0).astype(I32), far_ref, turn - 1)
        their_owner, their_within = block_of(lax.rem(rank + turn, splits))
        inside, ahead, count = running_order(their_owner == rank)
        send_ref[turn - 1 : turn, :] = slot_columns(
            inside, ahead, count, their_within, send_ref.shape[1]
        )


def middle_kernel(
    cap, splits, table_ref, map_ref, gate_ref, up_ref, turn_ref, near_ref, send_ref, far_ref, sent_ref,
    in_ref, own_ref, held_ref, key_ref, within_ref, in_sems, out_sems,
):
    layers, rows, narrow = gate_ref.shape
    loads = load_weights([0, layers - 1], gate_ref, up_ref, in_ref, in_sems)
    me = lax.axis_index("section")
    table = table_ref[...]
    column_plan(narrow, map_ref, near_ref, send_ref, far_ref, splits)
    scale = 1.0 / count_of(table, iota((rows, 1), 0) + me * rows)
    pick, count = pick_matrix(table, me, cap, key_ref, within_ref, list(range(table.shape[0])))
    parts = [
        (loads[0], in_ref.at[0, :, pl.ds(0, narrow)], 0),
        (loads[1], in_ref.at[0, :, pl.ds(narrow, sent_ref.shape[1] - narrow)], narrow),
    ]
    stores = put_slots(parts, pick, 1.0 / count, held_ref, (sent_ref,), out_sems)
    for side, load in enumerate(loads[2:]):
        load.wait()
        columns = in_ref[1, :, side * narrow : (side + 1) * narrow]
        own_ref[side * rows : (side + 1) * rows] = (columns.astype(F32) * scale).astype(BF16)
    for s in range(splits - 1):
        turn_ref[s] = onehot_dot(own_ref, send_ref[s : s + 1, :], narrow).astype(BF16)
    for store in stores:
        store.wait()


def middle(table, columns, gate, up, cap, splits, width, moved):
    _, rows, narrow = gate.shape
    blocks = table.shape[0]
    extra = columns.size // splits
    return pl.pallas_call(
        functools.partial(middle_kernel, cap, splits),
        out_shape=(
            jax.ShapeDtypeStruct((splits - 1, 2 * rows, width), BF16),
            jax.ShapeDtypeStruct((1, extra), I32),
            jax.ShapeDtypeStruct((splits - 1, width), I32),
            jax.ShapeDtypeStruct((splits - 1, extra), I32),
            jax.ShapeDtypeStruct((blocks * cap, 2 * narrow - moved), BF16),
        ),
        in_specs=[VMEM, VMEM, HBM, HBM],
        out_specs=(VMEM, VMEM, VMEM, VMEM, HBM),
        scratch_shapes=[
            pltpu.VMEM((2, rows, 2 * narrow), BF16),
            pltpu.VMEM((2 * rows, narrow), BF16),
            pltpu.VMEM((blocks * cap, 2 * narrow - moved), BF16),
            pltpu.VMEM((blocks, rows), I32),
            pltpu.VMEM((blocks, rows), I32),
            pltpu.SemaphoreType.DMA((2, 2)),
            pltpu.SemaphoreType.DMA((2, 1)),
        ],
        cost_estimate=pl.CostEstimate(
            flops=4 * rows * narrow * width,
            bytes_accessed=16 * rows * narrow,
            transcendentals=0,
        ),
        name="middle",
    )(table, columns, gate, up)


def land_kernel(cap, table_ref, land_ref):
    mine = table_ref[pl.ds(lax.axis_index("section"), 1), :]
    land_ref[...] = land_matrix(mine, table_ref.shape[0], cap)


def land_rows(table, cap):
    blocks, rows = table.shape
    return pl.pallas_call(
        functools.partial(land_kernel, cap),
        out_shape=jax.ShapeDtypeStruct((rows, blocks * cap), BF16),
        in_specs=[VMEM],
        out_specs=VMEM,
        compiler_params=PARAMS,
        name="land_rows",
    )(table)


def arrive_kernel(land_ref, ids_ref, *refs):
    *came_refs, rows_ref, rest_ref, gate_ref, up_ref, held_ref, sems = refs
    narrow = rows_ref.shape[1]
    rows = land_ref.shape[0]
    cap = came_refs[0].shape[0]
    me = lax.axis_index("section")
    starts = [me ^ p for p in range(len(came_refs))]
    loads = []
    for piece, (ref, start) in enumerate(zip(came_refs, starts)):
        where = pl.ds(pl.multiple_of(start * cap, cap), ref.shape[0])
        loads.append(pltpu.make_async_copy(ref, held_ref.at[where, :], sems.at[piece]))
        loads[-1].start()
    for load in loads:
        load.wait()
    for side in range(2):
        rows_ref[side * rows : (side + 1) * rows] = jnp.dot(
            land_ref[...],
            held_ref[:, side * narrow : (side + 1) * narrow],
            preferred_element_type=F32,
        ).astype(BF16)
    for s in range(ids_ref.shape[0]):
        picked = onehot_dot(rows_ref, ids_ref[s : s + 1, :], narrow).astype(BF16)
        gate_ref[s] = picked[:rows]
        up_ref[s] = picked[rows:]
    rest_ref[...] = jnp.dot(
        land_ref[...], held_ref[:, 2 * narrow :], preferred_element_type=F32
    ).astype(BF16)


def arrive_rows(land, ids, came, moved):
    rows, slots = land.shape
    narrow = (came[0].shape[1] - moved) // 2
    turns, width = ids.shape
    return pl.pallas_call(
        arrive_kernel,
        out_shape=(
            jax.ShapeDtypeStruct((2 * rows, narrow), BF16),
            jax.ShapeDtypeStruct((rows, moved), BF16),
            jax.ShapeDtypeStruct((turns, rows, width), BF16),
            jax.ShapeDtypeStruct((turns, rows, width), BF16),
        ),
        in_specs=[VMEM, VMEM] + [HBM] * len(came),
        out_specs=(VMEM,) * 4,
        scratch_shapes=[
            pltpu.VMEM((slots, 2 * narrow + moved), BF16),
            pltpu.SemaphoreType.DMA((len(came),)),
        ],
        compiler_params=PARAMS,
        cost_estimate=pl.CostEstimate(
            flops=4 * rows * narrow * width * turns,
            bytes_accessed=8 * rows * narrow,
            transcendentals=0,
        ),
        name="arrive_rows",
    )(land, ids, *came)


def near_kernel(rows_ref, ids_ref, out_ref):
    for start, size in column_tiles(ids_ref.shape[1]):
        out_ref[:, start : start + size] = onehot_dot(
            rows_ref, ids_ref[:, start : start + size], rows_ref.shape[1]
        ).astype(BF16)


def near_columns(rows, ids):
    count, narrow = rows.shape
    extra = ids.shape[1]
    return pl.pallas_call(
        near_kernel,
        out_shape=jax.ShapeDtypeStruct((count, extra), BF16),
        in_specs=[VMEM] * 2,
        out_specs=VMEM,
        compiler_params=PARAMS,
        cost_estimate=pl.CostEstimate(
            flops=2 * count * narrow * extra,
            bytes_accessed=2 * count * (narrow + extra),
            transcendentals=0,
        ),
    )(rows, ids)


def column_tiles(extent):
    pieces = -(-extent // 1408)
    size = extent // pieces // 256 * 256 or extent
    starts = [size * piece for piece in range(pieces)]
    return [
        (start, (extent if start == starts[-1] else start + size) - start) for start in starts
    ]


def put_extras(half, narrow, near, far_ref, ids_ref, outs, held_ref, sems):
    rows = held_ref.shape[0] // len(outs)
    layers = outs[0].shape[0]
    copies = []
    for step, (start, size) in enumerate(column_tiles(held_ref.shape[1])):
        total = None
        for s in range(ids_ref.shape[0]):
            far = onehot_dot(far_ref.at[s], ids_ref[s : s + 1, start : start + size], far_ref.shape[2])
            total = far if total is None else total + far
        held_ref[:, start : start + size] = (total + near(start, size)).astype(BF16)
        for layer in range(layers):
            for side, out in enumerate(outs):
                copies.append(
                    pltpu.make_async_copy(
                        held_ref.at[pl.ds(side * rows, rows), pl.ds(start, size)],
                        out.at[layer, half, :, pl.ds(narrow + start, size)],
                        sems.at[step, layer, side],
                    )
                )
                copies[-1].start()
    return copies


def first_kernel(
    table_ref, near_ids_ref, far_ref, far_ids_ref, gate_ref, up_ref, gate_out, up_out,
    in_ref, base_ref, held_ref, in_sems, base_sems, sems,
):
    layers, rows, narrow = gate_ref.shape
    order = list(range(layers))[::-1]
    loads = load_weights(order, gate_ref, up_ref, in_ref, in_sems)
    scale = 1.0 / count_of(
        table_ref[...], iota((rows, 1), 0) + lax.axis_index("section") * rows
    )
    outs = (gate_out, up_out)
    copies = []
    for number, load in enumerate(loads):
        at, side = number // 2, number % 2
        load.wait()
        here = pl.ds(side * rows, rows)
        columns = in_ref[at, :, side * narrow : (side + 1) * narrow]
        base_ref[at, here] = (columns.astype(F32) * scale).astype(BF16)
        copies.append(
            pltpu.make_async_copy(
                base_ref.at[at, here],
                outs[side].at[order[at], 0, :, pl.ds(0, narrow)],
                base_sems.at[at, side],
            )
        )
        copies[-1].start()

    def near(start, size):
        return onehot_dot(base_ref.at[0], near_ids_ref[:, start : start + size], narrow)

    copies += put_extras(0, narrow, near, far_ref, far_ids_ref, outs, held_ref, sems)
    for copy in copies:
        copy.wait()


def first_half(table, near_ids, far, far_ids, gate, up, out_type):
    layers, rows, narrow = gate.shape
    extra = near_ids.shape[1]
    return pl.pallas_call(
        first_kernel,
        out_shape=(out_type, out_type),
        in_specs=[VMEM] * 4 + [HBM] * 2,
        out_specs=(HBM, HBM),
        scratch_shapes=[
            pltpu.VMEM((layers, rows, 2 * narrow), BF16),
            pltpu.VMEM((layers, 2 * rows, narrow), BF16),
            pltpu.VMEM((2 * rows, extra), BF16),
            pltpu.SemaphoreType.DMA((layers, 2)),
            pltpu.SemaphoreType.DMA((layers, 2)),
            pltpu.SemaphoreType.DMA((len(column_tiles(extra)), layers, 2)),
        ],
        compiler_params=PARAMS,
        cost_estimate=pl.CostEstimate(
            flops=4 * rows * (narrow + far.shape[2] * far.shape[0]) * extra,
            bytes_accessed=8 * layers * rows * (narrow + extra),
            transcendentals=0,
        ),
        name="first_half",
    )(table, near_ids, far, far_ids, gate, up)


def second_kernel(with_rest, rows_ref, near_ref, far_ref, ids_ref, *refs):
    rest_ref, _, out_ref, held_ref, base_sems, sems = refs if with_rest else (None, *refs)
    narrow = rows_ref.shape[1]
    layers = out_ref.shape[0]
    copies = [
        pltpu.make_async_copy(
            rows_ref, out_ref.at[layers - 1, 1, :, pl.ds(0, narrow)], base_sems.at[0]
        )
    ]
    if with_rest:
        moved = rest_ref.shape[1]
        copies.append(
            pltpu.make_async_copy(
                rest_ref, out_ref.at[0, 1, :, pl.ds(narrow - moved, moved)], base_sems.at[1]
            )
        )
    for copy in copies:
        copy.start()

    def near(start, size):
        return near_ref[:, start : start + size].astype(F32)

    copies += put_extras(1, narrow, near, far_ref, ids_ref, (out_ref,), held_ref, sems)
    for copy in copies:
        copy.wait()


def second_half(rows, near, far, ids, rest, out, side):
    count, narrow = rows.shape[0] // 2, rows.shape[1]
    extra = near.shape[1]
    layers = out.shape[0]
    rests = [] if rest is None else [rest]
    return pl.pallas_call(
        functools.partial(second_kernel, bool(rests)),
        out_shape=jax.ShapeDtypeStruct(out.shape, BF16),
        grid=(1,),
        in_specs=[
            pl.BlockSpec((count, narrow), lambda i: (side, 0)),
            pl.BlockSpec((count, extra), lambda i: (side, 0)),
            pl.BlockSpec(far.shape, lambda i: (0, 0, 0)),
            pl.BlockSpec(ids.shape, lambda i: (0, 0)),
            *[pl.BlockSpec(array.shape, lambda i: (0, 0)) for array in rests],
            HBM,
        ],
        out_specs=HBM,
        input_output_aliases={4 + len(rests): 0},
        scratch_shapes=[
            pltpu.VMEM((count, extra), BF16),
            pltpu.SemaphoreType.DMA((2,)),
            pltpu.SemaphoreType.DMA((len(column_tiles(extra)), layers, 1)),
        ],
        compiler_params=PARAMS,
        cost_estimate=pl.CostEstimate(
            flops=2 * count * far.shape[2] * far.shape[0] * extra,
            bytes_accessed=4 * count * (narrow + layers * extra),
            transcendentals=0,
        ),
    )(rows, near, far, ids, *rests, out)


def last_pieces(narrow, total):
    return [
        (side, side * narrow + start, start, size)
        for side, extent in enumerate((narrow, total - narrow))
        for start, size in column_tiles(extent)
    ]


def last_kernel(narrow, land_ref, came_ref, gate_in, up_in, gate_out, up_out, held_ref, sems):
    outs = (gate_out, up_out)
    stores = []
    for number, (side, at, start, size) in enumerate(last_pieces(narrow, came_ref.shape[1])):
        held_ref[:, at : at + size] = jnp.dot(
            land_ref[...], came_ref[:, at : at + size], preferred_element_type=F32
        ).astype(BF16)
        stores.append(
            pltpu.make_async_copy(
                held_ref.at[:, pl.ds(at, size)],
                outs[side].at[0, 1, :, pl.ds(start, size)],
                sems.at[number],
            )
        )
        stores[-1].start()
    for store in stores:
        store.wait()


def last_rows(land, came, gate_out, up_out, narrow):
    rows, slots = land.shape
    total = came.shape[1]
    out_type = jax.ShapeDtypeStruct(gate_out.shape, BF16)
    return pl.pallas_call(
        functools.partial(last_kernel, narrow),
        out_shape=(out_type, out_type),
        in_specs=[VMEM] * 2 + [HBM] * 2,
        out_specs=(HBM, HBM),
        input_output_aliases={2: 0, 3: 1},
        scratch_shapes=[
            pltpu.VMEM((rows, total), BF16),
            pltpu.SemaphoreType.DMA((len(last_pieces(narrow, total)),)),
        ],
        compiler_params=PARAMS,
        cost_estimate=pl.CostEstimate(
            flops=2 * rows * slots * total,
            bytes_accessed=4 * rows * total,
            transcendentals=0,
        ),
        name="last_rows",
    )(land, came, gate_out, up_out)


def turn_around(sent, splits):
    return jnp.stack(
        [
            lax.ppermute(sent[turn - 1], "mp", [(i, (i + turn) % splits) for i in range(splits)])
            for turn in range(1, splits)
        ]
    )


def tiled_local(gate_weight, up_weight, hidden_map, ffn_map):
    layers, rows, narrow = gate_weight.shape
    blocks = lax.axis_size("section")
    splits = lax.axis_size("mp")
    extra = ffn_map.shape[0] // splits
    cap = rows // blocks
    column_cap = extra // splits
    width = -(-column_cap // 128) * 128
    moved = min(MOVED_TILES, narrow // 256) * 128
    table = hidden_map.reshape(blocks, rows)
    out_type = jax.ShapeDtypeStruct((layers, 2, rows, narrow + extra), BF16)

    def swap_rows(sent):
        return lax.all_to_all(sent, "section", split_axis=0, concat_axis=0, tiled=True)

    def cross(sent, p):
        return lax.ppermute(sent, "section", [(i, i ^ p) for i in range(blocks)])

    sent_top = send_rows(table, gate_weight, up_weight, layers - 1, cap, moved)
    came_top = [sent_top[0]] + [cross(sent_top[p], p) for p in range(1, blocks)]
    columns = ffn_map.reshape(-1, 128)
    own_sent, near_ids, send_ids, far_ids, sent_low = middle(
        table, columns, gate_weight, up_weight, cap, splits, width, moved
    )
    own_far = turn_around(own_sent, splits)
    came_low = swap_rows(sent_low)
    land = land_rows(table, cap)
    got, rest, *got_sent = arrive_rows(land, send_ids, came_top, moved)
    got_far = [turn_around(got_sent[side], splits) for side in range(2)]
    outs = first_half(table, near_ids, own_far, far_ids, gate_weight, up_weight, out_type)
    got_near = near_columns(got, near_ids)
    outs = [
        second_half(
            got, got_near, got_far[side], far_ids,
            rest if side else None, outs[side], side,
        )
        for side in range(2)
    ]
    return last_rows(land, came_low, *outs, narrow)


def plain_local(gate_weight, up_weight, hidden_map, ffn_map):
    layers, shard_rows, _ = gate_weight.shape
    blocks = lax.axis_size("section")
    splits = lax.axis_size("mp")
    section_rank = lax.axis_index("section")
    column_rank = lax.axis_index("mp")
    d_old = shard_rows * blocks
    extra_dev = ffn_map.shape[0] // splits
    route_cap = max(1, shard_rows // blocks)
    next_pick = jnp.minimum(jnp.arange(layers, dtype=jnp.int32) + 1, layers - 1) - 1
    counts = (
        jax.ops.segment_sum(jnp.ones((d_old,), jnp.float32), hidden_map, num_segments=d_old) + 1.0
    )
    own_rows = section_rank * shard_rows + jnp.arange(shard_rows, dtype=jnp.int32)
    copied = lax.dynamic_slice_in_dim(hidden_map, section_rank * shard_rows, shard_rows)
    mine_extra = lax.dynamic_slice_in_dim(ffn_map, column_rank * extra_dev, extra_dev)
    table = hidden_map.reshape(blocks, shard_rows)
    owner = table // shard_rows
    wanted = owner == section_rank
    order = jnp.cumsum(wanted.astype(jnp.int32), axis=1) - 1
    slot_ids = jnp.arange(route_cap, dtype=jnp.int32)
    selected = wanted[:, None, :] & (order[:, None, :] == slot_ids[None, :, None])
    sent_rows = jnp.sum(jnp.where(selected, (table % shard_rows)[:, None, :], 0), axis=2).reshape(
        -1
    )
    mine_owner = copied // shard_rows
    row_ids = jnp.arange(shard_rows, dtype=jnp.int32)
    earlier = row_ids[None, :] < row_ids[:, None]
    rank_among = jnp.sum(
        (earlier & (mine_owner[None, :] == mine_owner[:, None])).astype(jnp.int32), axis=1
    )
    landing = mine_owner * route_cap + rank_among
    pair = (gate_weight, up_weight)
    later = tuple((portion[1:] for portion in pair))
    rows_here = pair[0].shape[1]

    def pick_columns(carried, pieces):
        amount = pieces[0].shape[2]
        inside = (mine_extra >= 0) & (mine_extra < amount)
        bounded = jnp.clip(mine_extra, 0, amount - 1)
        return tuple(
            (
                jnp.where(inside, jnp.take(portion, bounded, axis=2), current)
                for current, portion in zip(carried, pieces)
            )
        )

    empty_extra = jnp.zeros((layers - 1, rows_here, extra_dev), jnp.bfloat16)
    extras = pick_columns(
        (empty_extra, empty_extra),
        (
            lax.all_gather(later[0], "mp", axis=2, tiled=True),
            lax.all_gather(later[1], "mp", axis=2, tiled=True),
        ),
    )
    own_gate, own_up = tuple(
        (
            jnp.concatenate([portion, added[next_pick]], axis=2)
            for portion, added in zip(pair, extras)
        )
    )
    arrived = (
        lax.all_to_all(
            jnp.take(own_gate, sent_rows, axis=1),
            "section",
            split_axis=1,
            concat_axis=1,
            tiled=True,
        ),
        lax.all_to_all(
            jnp.take(own_up, sent_rows, axis=1), "section", split_axis=1, concat_axis=1, tiled=True
        ),
    )
    grown_gate = jnp.stack([own_gate, jnp.take(arrived[0], landing, axis=1)], axis=1)
    grown_up = jnp.stack([own_up, jnp.take(arrived[1], landing, axis=1)], axis=1)
    divisor = jnp.stack([counts[own_rows], counts[copied]])[None, :, :, None]
    return (
        (grown_gate.astype(jnp.float32) / divisor).astype(jnp.bfloat16),
        (grown_up.astype(jnp.float32) / divisor).astype(jnp.bfloat16),
    )


def local(gate_weight, up_weight, hidden_map, ffn_map):
    layers, rows, narrow = gate_weight.shape
    blocks = lax.axis_size("section")
    splits = lax.axis_size("mp")
    extra = ffn_map.shape[0] // splits
    whole_tiles = (
        layers == 2
        and splits > 1
        and blocks > 1
        and blocks & (blocks - 1) == 0
        and rows % (8 * blocks) == 0
        and rows % 16 == 0
        and narrow % 256 == 0
        and extra % 128 == 0
        and extra % splits == 0
    )
    form = tiled_local if whole_tiles else plain_local
    return form(gate_weight, up_weight, hidden_map, ffn_map)


def solution(mesh):
    in_specs = (P(None, "section", "mp"), P(None, "section", "mp"), P(), P())
    out_specs = (P(None, None, "section", "mp"), P(None, None, "section", "mp"))
    return jax.shard_map(local, mesh=mesh, in_specs=in_specs, out_specs=out_specs, check_vma=False)
```

```python
import functools

import jax
import jax.numpy as jnp
from jax import lax
from jax.experimental import pallas as pl
from jax.experimental.pallas import tpu as pltpu
from jax.sharding import PartitionSpec as P


F32 = jnp.float32
BF16 = jnp.bfloat16
I32 = jnp.int32
VMEM = pl.BlockSpec(memory_space=pltpu.VMEM)
HBM = pl.BlockSpec(memory_space=pl.ANY)
K_CHUNK = 256
MOVED_TILES = 2
PARAMS = pltpu.CompilerParams(vmem_limit_bytes=32 << 20)


def iota(shape, axis):
    return lax.broadcasted_iota(I32, shape, axis)


def count_of(table, ids):
    total = jnp.zeros((ids.shape[0], table.shape[1]), F32)
    for block in range(table.shape[0]):
        total += jnp.where(table[block : block + 1, :] == ids, 1.0, 0.0)
    return 1.0 + jnp.sum(total, axis=1, keepdims=True)


def pick_matrix(table, me, cap, key_ref, within_ref, targets):
    blocks, rows = table.shape
    owner = lax.div(table, jnp.full_like(table, rows))
    within_ref[...] = table - owner * rows
    wanted = owner == me
    before = (iota((rows, rows), 0) < iota((rows, rows), 1)).astype(F32).astype(BF16)
    order = jnp.dot(wanted.astype(F32).astype(BF16), before, preferred_element_type=F32)
    key_ref[...] = jnp.where(wanted, order.astype(I32), -1)
    slot = iota((cap, rows), 0)
    parts = []
    for target in targets:
        line = pl.ds(target, 1)
        parts.append(jnp.where(key_ref[line, :] == slot, within_ref[line, :], 0).astype(F32))
    row_of = jnp.sum(jnp.concatenate(parts, axis=0), axis=1, keepdims=True).astype(I32)
    pick = (iota((blocks * cap, rows), 1) == row_of).astype(F32).astype(BF16)
    own = count_of(table, iota((rows, 1), 0) + me * rows)
    high = jnp.floor(own * (1.0 / 64.0))
    low = own - high * 64.0
    spread = [jnp.broadcast_to(part, (rows, 128)).astype(BF16) for part in (high, low)]
    high, low = [jnp.dot(pick, part, preferred_element_type=F32)[:, :1] for part in spread]
    return pick, high * 64.0 + low, own


def land_matrix(mine, blocks, cap):
    rows = mine.shape[1]
    across, down = iota((rows, rows), 1), iota((rows, rows), 0)
    column = jnp.sum(
        jnp.where(across == down, mine, 0).astype(F32), axis=1, keepdims=True
    ).astype(I32)
    owner_row = lax.div(mine, jnp.full_like(mine, rows))
    owner = lax.div(column, jnp.full_like(column, rows))
    earlier = (across < down) & (owner == owner_row)
    rank = jnp.sum(jnp.where(earlier, 1.0, 0.0), axis=1, keepdims=True).astype(I32)
    return (iota((rows, blocks * cap), 1) == owner * cap + rank).astype(F32).astype(BF16)


def onehot_dot(left, index_row, extent):
    total = None
    for start in range(0, extent, K_CHUNK):
        size = min(K_CHUNK, extent - start)
        mask = iota((size, index_row.shape[1]), 0) == index_row - start
        term = jnp.dot(
            left[:, start : start + size],
            mask.astype(F32).astype(BF16),
            preferred_element_type=F32,
        )
        total = term if total is None else total + term
    return total


def load_weights(layers, gate_ref, up_ref, in_ref, sems):
    narrow = gate_ref.shape[2]
    loads = []
    for at, layer in enumerate(layers):
        for side, ref in enumerate((gate_ref, up_ref)):
            loads.append(
                pltpu.make_async_copy(
                    ref.at[layer],
                    in_ref.at[at, :, pl.ds(side * narrow, narrow)],
                    sems.at[at, side],
                )
            )
            loads[-1].start()
    return loads


def put_slots(parts, pick, scale, held_ref, sent_refs, sems):
    stores = []
    for number, (load, source, start) in enumerate(parts):
        columns = pl.ds(start, source.shape[1])
        load.wait()
        rows = jnp.dot(pick, source[...], preferred_element_type=F32)
        held_ref[:, columns] = (rows * scale).astype(BF16)
        first = 0
        for piece, ref in enumerate(sent_refs):
            count = ref.shape[0]
            stores.append(
                pltpu.make_async_copy(
                    held_ref.at[pl.ds(first, count), columns],
                    ref.at[:, columns],
                    sems.at[number, piece],
                )
            )
            stores[-1].start()
            first += count
    return stores


def send_kernel(layer, cap, table_ref, gate_ref, up_ref, *refs):
    *sent_refs, map_ref, in_ref, rest_ref, held_ref, key_ref, within_ref = refs[:-4]
    map_sem, in_sems, rest_sem, out_sems = refs[-4:]
    narrow, moved = gate_ref.shape[2], rest_ref.shape[1]
    map_load = pltpu.make_async_copy(table_ref, map_ref, map_sem)
    map_load.start()
    loads = load_weights([layer], gate_ref, up_ref, in_ref, in_sems)
    rest = pltpu.make_async_copy(up_ref.at[0, :, pl.ds(narrow - moved, moved)], rest_ref, rest_sem)
    rest.start()
    me = lax.axis_index("section")
    targets = [me ^ p for p in range(map_ref.shape[0])]
    map_load.wait()
    pick, count, _ = pick_matrix(map_ref[...], me, cap, key_ref, within_ref, targets)
    parts = [
        (loads[0], in_ref.at[0, :, pl.ds(0, narrow)], 0),
        (loads[1], in_ref.at[0, :, pl.ds(narrow, narrow)], narrow),
        (rest, rest_ref, 2 * narrow),
    ]
    for store in put_slots(parts, pick, 1.0 / count, held_ref, sent_refs, out_sems):
        store.wait()


def send_rows(table, gate, up, layer, cap, moved):
    _, rows, narrow = gate.shape
    blocks = table.shape[0]
    return pl.pallas_call(
        functools.partial(send_kernel, layer, cap),
        out_shape=[jax.ShapeDtypeStruct((cap, 2 * narrow + moved), BF16)] * blocks,
        in_specs=[HBM] * 3,
        out_specs=[HBM] * blocks,
        scratch_shapes=[
            pltpu.VMEM((blocks, rows), I32),
            pltpu.VMEM((1, rows, 2 * narrow), BF16),
            pltpu.VMEM((rows, moved), BF16),
            pltpu.VMEM((blocks * cap, 2 * narrow + moved), BF16),
            pltpu.VMEM((blocks, rows), I32),
            pltpu.VMEM((blocks, rows), I32),
            pltpu.SemaphoreType.DMA(()),
            pltpu.SemaphoreType.DMA((1, 2)),
            pltpu.SemaphoreType.DMA(()),
            pltpu.SemaphoreType.DMA((3, blocks)),
        ],
        cost_estimate=pl.CostEstimate(
            flops=4 * blocks * cap * rows * narrow,
            bytes_accessed=8 * rows * narrow,
            transcendentals=0,
        ),
        name="send_rows",
    )(table, gate, up)


def running_order(hit):
    lines, lanes = hit.shape
    ones = hit.astype(F32)
    before = (iota((lanes, lanes), 0) < iota((lanes, lanes), 1)).astype(F32).astype(BF16)
    above = (iota((lines, lines), 1) < iota((lines, lines), 0)).astype(F32).astype(BF16)
    count = jnp.sum(ones, axis=1, keepdims=True)
    ahead = jnp.dot(
        above, jnp.broadcast_to(count, (lines, lanes)).astype(BF16), preferred_element_type=F32
    )[:, :1]
    inside = jnp.dot(ones.astype(BF16), before, preferred_element_type=F32)
    return jnp.where(hit, inside, -1.0), ahead, count


def slot_columns(inside, ahead, count, within, width):
    lines, _ = inside.shape
    slot = iota((lines, width), 1).astype(F32)
    chosen = (slot >= ahead) & (slot < ahead + count)
    spread = chosen.astype(F32).astype(BF16)
    first = jnp.sum(jnp.where(chosen, ahead, 0.0), axis=0, keepdims=True)
    used = jnp.sum(chosen.astype(F32), axis=0, keepdims=True)
    high = lax.div(within, jnp.full_like(within, 256))
    low = within - high * 256

    def over_slots(value):
        return lax.dot_general(
            value.astype(F32).astype(BF16),
            spread,
            (((0,), (0,)), ((), ())),
            preferred_element_type=F32,
        )

    order = slot[:1] - first
    hit = over_slots(inside) == order
    column = jnp.sum(
        jnp.where(hit, over_slots(high) * 256.0 + over_slots(low), 0.0), axis=0, keepdims=True
    )
    return jnp.where(used > 0.0, column, -1.0).astype(I32)


def column_plan(narrow, map_ref, near_ref, send_ref, far_ref, splits):
    rank = lax.axis_index("mp")
    lines = map_ref.shape[0] // splits
    lanes = map_ref.shape[1]
    blocks = [map_ref[split * lines : (split + 1) * lines, :] for split in range(splits)]

    def block_of(index):
        chosen = blocks[0]
        for split in range(1, splits):
            chosen = jnp.where(index == split, blocks[split], chosen)
        owner = lax.div(chosen, jnp.full_like(chosen, narrow))
        return owner, chosen - owner * narrow

    def flatten(value, ref, at):
        for line in range(lines):
            ref[at : at + 1, line * lanes : (line + 1) * lanes] = value[line : line + 1, :]

    owner, within = block_of(rank)
    flatten(jnp.where(owner == rank, within, -1), near_ref, 0)
    for turn in range(1, splits):
        hit = owner == lax.rem(rank + splits - turn, splits)
        inside, ahead, _ = running_order(hit)
        flatten(jnp.where(hit, inside + ahead, -1.0).astype(I32), far_ref, turn - 1)
        their_owner, their_within = block_of(lax.rem(rank + turn, splits))
        inside, ahead, count = running_order(their_owner == rank)
        send_ref[turn - 1 : turn, :] = slot_columns(
            inside, ahead, count, their_within, send_ref.shape[1]
        )


def middle_kernel(
    cap, splits, table_ref, map_ref, gate_ref, up_ref, turn_ref, near_ref, send_ref, far_ref, sent_ref,
    in_ref, own_ref, held_ref, key_ref, within_ref, in_sems, out_sems,
):
    layers, rows, narrow = gate_ref.shape
    loads = load_weights([0, layers - 1], gate_ref, up_ref, in_ref, in_sems)
    me = lax.axis_index("section")
    table = table_ref[...]
    column_plan(narrow, map_ref, near_ref, send_ref, far_ref, splits)
    pick, count, own = pick_matrix(table, me, cap, key_ref, within_ref, list(range(table.shape[0])))
    scale = 1.0 / own
    parts = [
        (loads[0], in_ref.at[0, :, pl.ds(0, narrow)], 0),
        (loads[1], in_ref.at[0, :, pl.ds(narrow, sent_ref.shape[1] - narrow)], narrow),
    ]
    stores = put_slots(parts, pick, 1.0 / count, held_ref, (sent_ref,), out_sems)
    for side, load in enumerate(loads[2:]):
        load.wait()
        columns = in_ref[1, :, side * narrow : (side + 1) * narrow]
        own_ref[side * rows : (side + 1) * rows] = (columns.astype(F32) * scale).astype(BF16)
    for s in range(splits - 1):
        turn_ref[s] = onehot_dot(own_ref, send_ref[s : s + 1, :], narrow).astype(BF16)
    for store in stores:
        store.wait()


def middle(table, columns, gate, up, cap, splits, width, moved):
    _, rows, narrow = gate.shape
    blocks = table.shape[0]
    extra = columns.size // splits
    return pl.pallas_call(
        functools.partial(middle_kernel, cap, splits),
        out_shape=(
            jax.ShapeDtypeStruct((splits - 1, 2 * rows, width), BF16),
            jax.ShapeDtypeStruct((1, extra), I32),
            jax.ShapeDtypeStruct((splits - 1, width), I32),
            jax.ShapeDtypeStruct((splits - 1, extra), I32),
            jax.ShapeDtypeStruct((blocks * cap, 2 * narrow - moved), BF16),
        ),
        in_specs=[VMEM, VMEM, HBM, HBM],
        out_specs=(VMEM, VMEM, VMEM, VMEM, HBM),
        scratch_shapes=[
            pltpu.VMEM((2, rows, 2 * narrow), BF16),
            pltpu.VMEM((2 * rows, narrow), BF16),
            pltpu.VMEM((blocks * cap, 2 * narrow - moved), BF16),
            pltpu.VMEM((blocks, rows), I32),
            pltpu.VMEM((blocks, rows), I32),
            pltpu.SemaphoreType.DMA((2, 2)),
            pltpu.SemaphoreType.DMA((2, 1)),
        ],
        cost_estimate=pl.CostEstimate(
            flops=4 * rows * narrow * width,
            bytes_accessed=16 * rows * narrow,
            transcendentals=0,
        ),
        name="middle",
    )(table, columns, gate, up)


def land_kernel(cap, table_ref, land_ref):
    mine = table_ref[pl.ds(lax.axis_index("section"), 1), :]
    land_ref[...] = land_matrix(mine, table_ref.shape[0], cap)


def land_rows(table, cap):
    blocks, rows = table.shape
    return pl.pallas_call(
        functools.partial(land_kernel, cap),
        out_shape=jax.ShapeDtypeStruct((rows, blocks * cap), BF16),
        in_specs=[VMEM],
        out_specs=VMEM,
        compiler_params=PARAMS,
        name="land_rows",
    )(table)


def arrive_kernel(land_ref, ids_ref, *refs):
    *came_refs, rows_ref, rest_ref, gate_ref, up_ref, held_ref, sems = refs
    narrow = rows_ref.shape[1]
    rows = land_ref.shape[0]
    cap = came_refs[0].shape[0]
    me = lax.axis_index("section")
    starts = [me ^ p for p in range(len(came_refs))]
    loads = []
    for piece, (ref, start) in enumerate(zip(came_refs, starts)):
        where = pl.ds(pl.multiple_of(start * cap, cap), ref.shape[0])
        loads.append(pltpu.make_async_copy(ref, held_ref.at[where, :], sems.at[piece]))
        loads[-1].start()
    for load in loads:
        load.wait()
    for side in range(2):
        rows_ref[side * rows : (side + 1) * rows] = jnp.dot(
            land_ref[...],
            held_ref[:, side * narrow : (side + 1) * narrow],
            preferred_element_type=F32,
        ).astype(BF16)
    for s in range(ids_ref.shape[0]):
        picked = onehot_dot(rows_ref, ids_ref[s : s + 1, :], narrow).astype(BF16)
        gate_ref[s] = picked[:rows]
        up_ref[s] = picked[rows:]
    rest_ref[...] = jnp.dot(
        land_ref[...], held_ref[:, 2 * narrow :], preferred_element_type=F32
    ).astype(BF16)


def arrive_rows(land, ids, came, moved):
    rows, slots = land.shape
    narrow = (came[0].shape[1] - moved) // 2
    turns, width = ids.shape
    return pl.pallas_call(
        arrive_kernel,
        out_shape=(
            jax.ShapeDtypeStruct((2 * rows, narrow), BF16),
            jax.ShapeDtypeStruct((rows, moved), BF16),
            jax.ShapeDtypeStruct((turns, rows, width), BF16),
            jax.ShapeDtypeStruct((turns, rows, width), BF16),
        ),
        in_specs=[VMEM, VMEM] + [HBM] * len(came),
        out_specs=(VMEM,) * 4,
        scratch_shapes=[
            pltpu.VMEM((slots, 2 * narrow + moved), BF16),
            pltpu.SemaphoreType.DMA((len(came),)),
        ],
        compiler_params=PARAMS,
        cost_estimate=pl.CostEstimate(
            flops=4 * rows * narrow * width * turns,
            bytes_accessed=8 * rows * narrow,
            transcendentals=0,
        ),
        name="arrive_rows",
    )(land, ids, *came)


def near_kernel(rows_ref, ids_ref, out_ref):
    for start, size in column_tiles(ids_ref.shape[1]):
        out_ref[:, start : start + size] = onehot_dot(
            rows_ref, ids_ref[:, start : start + size], rows_ref.shape[1]
        ).astype(BF16)


def near_columns(rows, ids):
    count, narrow = rows.shape
    extra = ids.shape[1]
    return pl.pallas_call(
        near_kernel,
        out_shape=jax.ShapeDtypeStruct((count, extra), BF16),
        in_specs=[VMEM] * 2,
        out_specs=VMEM,
        compiler_params=PARAMS,
        cost_estimate=pl.CostEstimate(
            flops=2 * count * narrow * extra,
            bytes_accessed=2 * count * (narrow + extra),
            transcendentals=0,
        ),
    )(rows, ids)


def column_tiles(extent):
    pieces = -(-extent // 1408)
    size = extent // pieces // 256 * 256 or extent
    starts = [size * piece for piece in range(pieces)]
    return [
        (start, (extent if start == starts[-1] else start + size) - start) for start in starts
    ]


def put_extras(half, narrow, near, far_ref, ids_ref, outs, held_ref, sems):
    rows = held_ref.shape[0] // len(outs)
    layers = outs[0].shape[0]
    copies = []
    for step, (start, size) in enumerate(column_tiles(held_ref.shape[1])):
        total = None
        for s in range(ids_ref.shape[0]):
            far = onehot_dot(far_ref.at[s], ids_ref[s : s + 1, start : start + size], far_ref.shape[2])
            total = far if total is None else total + far
        held_ref[:, start : start + size] = (total + near(start, size)).astype(BF16)
        for layer in range(layers):
            for side, out in enumerate(outs):
                copies.append(
                    pltpu.make_async_copy(
                        held_ref.at[pl.ds(side * rows, rows), pl.ds(start, size)],
                        out.at[layer, half, :, pl.ds(narrow + start, size)],
                        sems.at[step, layer, side],
                    )
                )
                copies[-1].start()
    return copies


def first_kernel(
    table_ref, near_ids_ref, far_ref, far_ids_ref, gate_ref, up_ref, gate_out, up_out,
    in_ref, base_ref, held_ref, in_sems, base_sems, sems,
):
    layers, rows, narrow = gate_ref.shape
    order = list(range(layers))[::-1]
    loads = load_weights(order, gate_ref, up_ref, in_ref, in_sems)
    scale = 1.0 / count_of(
        table_ref[...], iota((rows, 1), 0) + lax.axis_index("section") * rows
    )
    outs = (gate_out, up_out)
    copies = []
    for number, load in enumerate(loads):
        at, side = number // 2, number % 2
        load.wait()
        here = pl.ds(side * rows, rows)
        columns = in_ref[at, :, side * narrow : (side + 1) * narrow]
        base_ref[at, here] = (columns.astype(F32) * scale).astype(BF16)
        copies.append(
            pltpu.make_async_copy(
                base_ref.at[at, here],
                outs[side].at[order[at], 0, :, pl.ds(0, narrow)],
                base_sems.at[at, side],
            )
        )
        copies[-1].start()

    def near(start, size):
        return onehot_dot(base_ref.at[0], near_ids_ref[:, start : start + size], narrow)

    copies += put_extras(0, narrow, near, far_ref, far_ids_ref, outs, held_ref, sems)
    for copy in copies:
        copy.wait()


def first_half(table, near_ids, far, far_ids, gate, up, out_type):
    layers, rows, narrow = gate.shape
    extra = near_ids.shape[1]
    return pl.pallas_call(
        first_kernel,
        out_shape=(out_type, out_type),
        in_specs=[VMEM] * 4 + [HBM] * 2,
        out_specs=(HBM, HBM),
        scratch_shapes=[
            pltpu.VMEM((layers, rows, 2 * narrow), BF16),
            pltpu.VMEM((layers, 2 * rows, narrow), BF16),
            pltpu.VMEM((2 * rows, extra), BF16),
            pltpu.SemaphoreType.DMA((layers, 2)),
            pltpu.SemaphoreType.DMA((layers, 2)),
            pltpu.SemaphoreType.DMA((len(column_tiles(extra)), layers, 2)),
        ],
        compiler_params=PARAMS,
        cost_estimate=pl.CostEstimate(
            flops=4 * rows * (narrow + far.shape[2] * far.shape[0]) * extra,
            bytes_accessed=8 * layers * rows * (narrow + extra),
            transcendentals=0,
        ),
        name="first_half",
    )(table, near_ids, far, far_ids, gate, up)


def second_kernel(with_rest, rows_ref, near_ref, far_ref, ids_ref, *refs):
    rest_ref, _, out_ref, held_ref, base_sems, sems = refs if with_rest else (None, *refs)
    narrow = rows_ref.shape[1]
    layers = out_ref.shape[0]
    copies = [
        pltpu.make_async_copy(
            rows_ref, out_ref.at[layers - 1, 1, :, pl.ds(0, narrow)], base_sems.at[0]
        )
    ]
    if with_rest:
        moved = rest_ref.shape[1]
        copies.append(
            pltpu.make_async_copy(
                rest_ref, out_ref.at[0, 1, :, pl.ds(narrow - moved, moved)], base_sems.at[1]
            )
        )
    for copy in copies:
        copy.start()

    def near(start, size):
        return near_ref[:, start : start + size].astype(F32)

    copies += put_extras(1, narrow, near, far_ref, ids_ref, (out_ref,), held_ref, sems)
    for copy in copies:
        copy.wait()


def second_half(rows, near, far, ids, rest, out, side):
    count, narrow = rows.shape[0] // 2, rows.shape[1]
    extra = near.shape[1]
    layers = out.shape[0]
    rests = [] if rest is None else [rest]
    return pl.pallas_call(
        functools.partial(second_kernel, bool(rests)),
        out_shape=jax.ShapeDtypeStruct(out.shape, BF16),
        grid=(1,),
        in_specs=[
            pl.BlockSpec((count, narrow), lambda i: (side, 0)),
            pl.BlockSpec((count, extra), lambda i: (side, 0)),
            pl.BlockSpec(far.shape, lambda i: (0, 0, 0)),
            pl.BlockSpec(ids.shape, lambda i: (0, 0)),
            *[pl.BlockSpec(array.shape, lambda i: (0, 0)) for array in rests],
            HBM,
        ],
        out_specs=HBM,
        input_output_aliases={4 + len(rests): 0},
        scratch_shapes=[
            pltpu.VMEM((count, extra), BF16),
            pltpu.SemaphoreType.DMA((2,)),
            pltpu.SemaphoreType.DMA((len(column_tiles(extra)), layers, 1)),
        ],
        compiler_params=PARAMS,
        cost_estimate=pl.CostEstimate(
            flops=2 * count * far.shape[2] * far.shape[0] * extra,
            bytes_accessed=4 * count * (narrow + layers * extra),
            transcendentals=0,
        ),
    )(rows, near, far, ids, *rests, out)


def last_pieces(narrow, total):
    return [
        (side, side * narrow + start, start, size)
        for side, extent in enumerate((narrow, total - narrow))
        for start, size in column_tiles(extent)
    ]


def last_kernel(narrow, land_ref, came_ref, gate_in, up_in, gate_out, up_out, held_ref, sems):
    outs = (gate_out, up_out)
    stores = []
    for number, (side, at, start, size) in enumerate(last_pieces(narrow, came_ref.shape[1])):
        held_ref[:, at : at + size] = jnp.dot(
            land_ref[...], came_ref[:, at : at + size], preferred_element_type=F32
        ).astype(BF16)
        stores.append(
            pltpu.make_async_copy(
                held_ref.at[:, pl.ds(at, size)],
                outs[side].at[0, 1, :, pl.ds(start, size)],
                sems.at[number],
            )
        )
        stores[-1].start()
    for store in stores:
        store.wait()


def last_rows(land, came, gate_out, up_out, narrow):
    rows, slots = land.shape
    total = came.shape[1]
    out_type = jax.ShapeDtypeStruct(gate_out.shape, BF16)
    return pl.pallas_call(
        functools.partial(last_kernel, narrow),
        out_shape=(out_type, out_type),
        in_specs=[VMEM] * 2 + [HBM] * 2,
        out_specs=(HBM, HBM),
        input_output_aliases={2: 0, 3: 1},
        scratch_shapes=[
            pltpu.VMEM((rows, total), BF16),
            pltpu.SemaphoreType.DMA((len(last_pieces(narrow, total)),)),
        ],
        compiler_params=PARAMS,
        cost_estimate=pl.CostEstimate(
            flops=2 * rows * slots * total,
            bytes_accessed=4 * rows * total,
            transcendentals=0,
        ),
        name="last_rows",
    )(land, came, gate_out, up_out)


def turn_around(sent, splits):
    return jnp.stack(
        [
            lax.ppermute(sent[turn - 1], "mp", [(i, (i + turn) % splits) for i in range(splits)])
            for turn in range(1, splits)
        ]
    )


def tiled_local(gate_weight, up_weight, hidden_map, ffn_map):
    layers, rows, narrow = gate_weight.shape
    blocks = lax.axis_size("section")
    splits = lax.axis_size("mp")
    extra = ffn_map.shape[0] // splits
    cap = rows // blocks
    column_cap = extra // splits
    width = -(-column_cap // 128) * 128
    moved = min(MOVED_TILES, narrow // 256) * 128
    table = hidden_map.reshape(blocks, rows)
    out_type = jax.ShapeDtypeStruct((layers, 2, rows, narrow + extra), BF16)

    def swap_rows(sent):
        return lax.all_to_all(sent, "section", split_axis=0, concat_axis=0, tiled=True)

    def cross(sent, p):
        return lax.ppermute(sent, "section", [(i, i ^ p) for i in range(blocks)])

    sent_top = send_rows(table, gate_weight, up_weight, layers - 1, cap, moved)
    came_top = [sent_top[0]] + [cross(sent_top[p], p) for p in range(1, blocks)]
    columns = ffn_map.reshape(-1, 128)
    own_sent, near_ids, send_ids, far_ids, sent_low = middle(
        table, columns, gate_weight, up_weight, cap, splits, width, moved
    )
    own_far = turn_around(own_sent, splits)
    came_low = swap_rows(sent_low)
    land = land_rows(table, cap)
    got, rest, *got_sent = arrive_rows(land, send_ids, came_top, moved)
    got_far = [turn_around(got_sent[side], splits) for side in range(2)]
    outs = first_half(table, near_ids, own_far, far_ids, gate_weight, up_weight, out_type)
    got_near = near_columns(got, near_ids)
    outs = [
        second_half(
            got, got_near, got_far[side], far_ids,
            rest if side else None, outs[side], side,
        )
        for side in range(2)
    ]
    return last_rows(land, came_low, *outs, narrow)


def plain_local(gate_weight, up_weight, hidden_map, ffn_map):
    layers, shard_rows, _ = gate_weight.shape
    blocks = lax.axis_size("section")
    splits = lax.axis_size("mp")
    section_rank = lax.axis_index("section")
    column_rank = lax.axis_index("mp")
    d_old = shard_rows * blocks
    extra_dev = ffn_map.shape[0] // splits
    route_cap = max(1, shard_rows // blocks)
    next_pick = jnp.minimum(jnp.arange(layers, dtype=jnp.int32) + 1, layers - 1) - 1
    counts = (
        jax.ops.segment_sum(jnp.ones((d_old,), jnp.float32), hidden_map, num_segments=d_old) + 1.0
    )
    own_rows = section_rank * shard_rows + jnp.arange(shard_rows, dtype=jnp.int32)
    copied = lax.dynamic_slice_in_dim(hidden_map, section_rank * shard_rows, shard_rows)
    mine_extra = lax.dynamic_slice_in_dim(ffn_map, column_rank * extra_dev, extra_dev)
    table = hidden_map.reshape(blocks, shard_rows)
    owner = table // shard_rows
    wanted = owner == section_rank
    order = jnp.cumsum(wanted.astype(jnp.int32), axis=1) - 1
    slot_ids = jnp.arange(route_cap, dtype=jnp.int32)
    selected = wanted[:, None, :] & (order[:, None, :] == slot_ids[None, :, None])
    sent_rows = jnp.sum(jnp.where(selected, (table % shard_rows)[:, None, :], 0), axis=2).reshape(
        -1
    )
    mine_owner = copied // shard_rows
    row_ids = jnp.arange(shard_rows, dtype=jnp.int32)
    earlier = row_ids[None, :] < row_ids[:, None]
    rank_among = jnp.sum(
        (earlier & (mine_owner[None, :] == mine_owner[:, None])).astype(jnp.int32), axis=1
    )
    landing = mine_owner * route_cap + rank_among
    pair = (gate_weight, up_weight)
    later = tuple((portion[1:] for portion in pair))
    rows_here = pair[0].shape[1]

    def pick_columns(carried, pieces):
        amount = pieces[0].shape[2]
        inside = (mine_extra >= 0) & (mine_extra < amount)
        bounded = jnp.clip(mine_extra, 0, amount - 1)
        return tuple(
            (
                jnp.where(inside, jnp.take(portion, bounded, axis=2), current)
                for current, portion in zip(carried, pieces)
            )
        )

    empty_extra = jnp.zeros((layers - 1, rows_here, extra_dev), jnp.bfloat16)
    extras = pick_columns(
        (empty_extra, empty_extra),
        (
            lax.all_gather(later[0], "mp", axis=2, tiled=True),
            lax.all_gather(later[1], "mp", axis=2, tiled=True),
        ),
    )
    own_gate, own_up = tuple(
        (
            jnp.concatenate([portion, added[next_pick]], axis=2)
            for portion, added in zip(pair, extras)
        )
    )
    arrived = (
        lax.all_to_all(
            jnp.take(own_gate, sent_rows, axis=1),
            "section",
            split_axis=1,
            concat_axis=1,
            tiled=True,
        ),
        lax.all_to_all(
            jnp.take(own_up, sent_rows, axis=1), "section", split_axis=1, concat_axis=1, tiled=True
        ),
    )
    grown_gate = jnp.stack([own_gate, jnp.take(arrived[0], landing, axis=1)], axis=1)
    grown_up = jnp.stack([own_up, jnp.take(arrived[1], landing, axis=1)], axis=1)
    divisor = jnp.stack([counts[own_rows], counts[copied]])[None, :, :, None]
    return (
        (grown_gate.astype(jnp.float32) / divisor).astype(jnp.bfloat16),
        (grown_up.astype(jnp.float32) / divisor).astype(jnp.bfloat16),
    )


def local(gate_weight, up_weight, hidden_map, ffn_map):
    layers, rows, narrow = gate_weight.shape
    blocks = lax.axis_size("section")
    splits = lax.axis_size("mp")
    extra = ffn_map.shape[0] // splits
    whole_tiles = (
        layers == 2
        and splits > 1
        and blocks > 1
        and blocks & (blocks - 1) == 0
        and rows % (8 * blocks) == 0
        and rows % 16 == 0
        and narrow % 256 == 0
        and extra % 128 == 0
        and extra % splits == 0
    )
    form = tiled_local if whole_tiles else plain_local
    return form(gate_weight, up_weight, hidden_map, ffn_map)


def solution(mesh):
    in_specs = (P(None, "section", "mp"), P(None, "section", "mp"), P(), P())
    out_specs = (P(None, None, "section", "mp"), P(None, None, "section", "mp"))
    return jax.shard_map(local, mesh=mesh, in_specs=in_specs, out_specs=out_specs, check_vma=False)
```
